512 devices in a mesh: pts: 128 (over x, z, y_lo, core), lmk: 4 (over y_hi).
Axes of the slice: x: 4, y: 8 (y_hi: 4, y_lo: 2; y = y_hi * 2 + y_lo), z: 8, core: 2. Of those that a mesh axis runs over, the one named last changes fastest.
Arguments:
- points: bfloat16 [32768, 768], P('pts'), may hold values from -6 to 6
- landmarks: bfloat16 [384, 768], P('lmk'), may hold values from -6 to 6
- panels: bfloat16 [128, 384, 2048], P('pts', None, 'lmk'), may hold values from -0.3125 to 0.3125
- panel_index: int32 [1], replicated, may hold values from 0 to 127
- assignment: int32 [32768], P('pts'), may hold values from 0 to 4095, as said below
Outputs:
- centroid_sums: float32 [4096, 2048], P('pts', 'lmk')
- cluster_counts: int32 [4096], P('pts')
The draws below stay inside these ranges and needn't reach their ends.
Inputs may be any that keep to these rules, and one draw needn't show every extreme that they name: `assignment`: owner of a cluster c is c // 32. In each aligned block of 256 points (the points of one device) at most 4 points have clusters of one owner; one owner, the same for every block, has exactly 4 points in every block.
All inputs are finite; a program needn't handle non-finite values.
Results may differ from the reference program's by a relative error of at most 0.0017.
Values may be sent and summed in bfloat16 or wider, within the bound.
A program may use at most 64 MiB of HBM per device.

```python
import math
import jax
import jax.numpy as jnp
from jax import lax

D = 768
FEAT = 2048
CLUSTERS = 4096
P_DEV = 256
NPTS = 32768
LMK = 384
PANELS = 128
CL_DEV = 32
CAP = 4
N_PTS = 128


def draw_assignment(key, part):
    key_hot = jax.random.fold_in(key, 11)
    key_blocks = jax.random.fold_in(key, 23)
    hot_owner = jax.random.randint(key_hot, (), 0, N_PTS).astype(jnp.int32)

    def one_block(block_key):
        key_slots = jax.random.fold_in(block_key, 1)
        key_order = jax.random.fold_in(block_key, 2)
        key_within = jax.random.fold_in(block_key, 3)
        slot_ids = jax.random.permutation(key_slots, (N_PTS - 1) * CAP)[:P_DEV - CAP].astype(jnp.int32)
        others = slot_ids // CAP
        others = others + (others >= hot_owner).astype(jnp.int32)
        owners = jnp.concatenate([jnp.full((CAP,), 1, jnp.int32) * hot_owner, others])
        owners = owners[jax.random.permutation(key_order, P_DEV)]
        within = jax.random.randint(key_within, (P_DEV,), 0, CL_DEV).astype(jnp.int32)
        return owners * CL_DEV + within
    block_keys = jax.random.split(key_blocks, N_PTS)
    return jax.vmap(one_block)(block_keys).reshape(-1)


def level_of(own_key, shape, pieces, least, top_value):
    level, own = 1.0, jax.random.fold_in(own_key, 6)
    for axis_at, parts in pieces:
        steps = jnp.exp(jax.random.uniform(jax.random.fold_in(own, axis_at), (parts,), jnp.float32, least / len(pieces), top_value / len(pieces)))
        level = level * jnp.repeat(steps, shape[axis_at] // parts).reshape([-1 if axis == axis_at else 1 for axis in range(len(shape))])
    return level


def gaussian(key, dims, width, limit, shards=(), kind=jnp.bfloat16):
    gain = level_of(key, dims, shards, -0.22, 0.18) if shards else 1.0
    values = jax.random.normal(key, dims, jnp.float32) * width * gain
    return jnp.minimum(jnp.maximum(values, -limit), limit).astype(kind)


def setup_inputs(seed: int = 0) -> dict:
    seeds = jax.random.split(jax.random.key(seed), 6)
    return {
        "points": gaussian(seeds[0], (NPTS, D), 1.0, 6.0, ((0, 128),)),
        "landmarks": gaussian(seeds[1], (LMK, D), 1.0, 6.0, ((0, 4),)),
        "panels": gaussian(seeds[2], (PANELS, LMK, FEAT), LMK ** -0.5, 0.3125, ((0, 128), (2, 4))),
        "panel_index": jax.random.randint(seeds[3], (1,), 0, PANELS).astype(jnp.int32),
        "assignment": draw_assignment(jax.random.fold_in(seeds[5], 71), 0),
    }


def unit_rows(values_in):
    widened = values_in.astype(jnp.float32)
    scale = lax.rsqrt(lax.optimization_barrier(jnp.mean(widened * widened, axis=1, keepdims=True)) + 1e-06)
    return (widened * scale).astype(jnp.bfloat16)

def kernel_rows(unit_points, unit_marks):
    scores = lax.dot_general(unit_points, unit_marks, (((1,), (1,)), ((), ())), preferred_element_type=jnp.float32)
    return jnp.exp(scores * (0.5 / math.sqrt(unit_points.shape[1]))).astype(jnp.bfloat16)

def reference(points, landmarks, panels, panel_index, assignment):
    unit_marks = unit_rows(landmarks)
    factor_panel = lax.dynamic_index_in_dim(panels, panel_index[0], 0, keepdims=False)

    def block_step(carry, block_index):
        totals, counts = carry
        first_row = (block_index * P_DEV).astype(jnp.int32)
        block_points = lax.dynamic_slice_in_dim(points, first_row, P_DEV, 0)
        block_ids = lax.dynamic_slice_in_dim(assignment, first_row, P_DEV, 0)
        kernel = kernel_rows(unit_rows(block_points), unit_marks)
        features = jnp.dot(kernel, factor_panel, preferred_element_type=jnp.float32).astype(jnp.bfloat16)
        totals = totals + jax.ops.segment_sum(features.astype(jnp.float32), block_ids, CLUSTERS)
        counts = counts + jax.ops.segment_sum(jnp.ones((P_DEV,), jnp.int32), block_ids, CLUSTERS)
        return ((totals, counts), None)
    start = (jnp.zeros((CLUSTERS, FEAT), jnp.float32), jnp.zeros((CLUSTERS,), jnp.int32))
    (totals, counts), unused = lax.scan(block_step, start, jnp.arange(N_PTS, dtype=jnp.int32))
    return (totals / (NPTS / CLUSTERS), counts)
```

```python
import functools
import math

import jax
import jax.numpy as jnp
from jax import lax
from jax.experimental import pallas as pl
from jax.experimental.pallas import tpu as pltpu
from jax.sharding import PartitionSpec as P

MESH = pl.DeviceIdType.MESH
CAP = 4
OWNED = 32
F32, BF16, I32 = jnp.float32, jnp.bfloat16, jnp.int32


def iota(shape, dim):
    return lax.broadcasted_iota(I32, shape, dim)


def dot(a, b, ca=1, cb=0):
    return lax.dot_general(a, b, (((ca,), (cb,)), ((), ())), preferred_element_type=F32)


def unit_rows(values):
    wide = values.astype(F32)
    scale = lax.rsqrt(jnp.mean(wide * wide, axis=1, keepdims=True) + 1e-06)
    return (wide * scale).astype(BF16)


def kernel(
    nx,
    nz,
    nl,
    index_ref,
    points_hbm,
    marks_hbm,
    panel_hbm,
    assign_hbm,
    out_ref,
    count_ref,
    points,
    marks,
    assign,
    slots,
    rows_z,
    regrouped,
    rows_q,
    pieces,
    planes,
    panel,
    sums,
    load_sem,
    rz_send,
    rz_recv,
    rq_send,
    rq_recv,
    p1_send,
    p1_recv,
    p2_send,
    p2_recv,
    p3_send,
    p3_recv,
    s_send,
    s_recv,
):
    nq = nx * 4
    me, my_l = lax.axis_index("pts"), lax.axis_index("lmk")
    my_x, my_z, my_yc = me // (nz * 4), (me // 4) % nz, me % 4
    my_y, my_c = my_yc // 2, my_yc % 2
    my_q = my_x * 4 + my_yc
    n_marks, depth = marks_hbm.shape
    n_points = points_hbm.shape[0]

    plane_peers = []
    for dx in range(nx):
        for dy in range(2):
            for dc in range(2):
                if dx or dy or dc:
                    x = (my_x + dx) % nx
                    yc = (my_y + dy) % 2 * 2 + (my_c + dc) % 2
                    plane_peers.append((x * 4 + yc, ((x * nz + my_z) * 4 + yc, my_l)))
    z_peers = []
    for dz in range(1, nz):
        z = (my_z + dz) % nz
        z_peers.append((z, ((my_x * nz + z) * 4 + my_yc, my_l)))
    l_peers = []
    for dl in range(1, nl):
        l = (my_l + dl) % nl
        l_peers.append((l, (me, l)))

    def piece_of(q):
        rows = pl.ds(pl.multiple_of(q // 4 * n_marks, n_marks), n_marks)
        return panel_hbm.at[0, rows, pl.ds(pl.multiple_of(q % 4 * 128, 128), 128)]

    loads = [
        pltpu.make_async_copy(points_hbm, points, load_sem.at[0]),
        pltpu.make_async_copy(marks_hbm, marks.at[pl.ds(0, n_marks)], load_sem.at[1]),
        pltpu.make_async_copy(assign_hbm, assign, load_sem.at[2]),
        pltpu.make_async_copy(piece_of(my_q), pieces.at[my_q], load_sem.at[3]),
    ]
    barrier = pltpu.get_barrier_semaphore()
    everyone = plane_peers + z_peers + l_peers
    for _, device in everyone:
        pl.semaphore_signal(barrier, inc=1, device_id=device, device_id_type=MESH)
    for load in loads:
        load.start()

    def remote(src, dst, send, recv, device):
        return pltpu.make_async_remote_copy(
            src_ref=src,
            dst_ref=dst,
            send_sem=send,
            recv_sem=recv,
            device_id=device,
            device_id_type=MESH,
        )

    marks[n_marks:, :] = jnp.zeros((128 - n_marks, depth), BF16)
    loads[2].wait()
    assigned = assign[...]
    owner, local = assigned // OWNED, assigned % OWNED
    n_owners = nq * nz
    hits = iota((n_owners, n_points), 0) == owner
    earlier = (iota((n_points, n_points), 0) < iota((n_points, n_points), 1)).astype(F32)
    before = dot(hits.astype(BF16), earlier.astype(BF16))
    rank = jnp.sum(jnp.where(hits, before, 0.0), axis=0, keepdims=True).astype(I32)
    owner_q = owner // (nz * 4) * 4 + owner % 4
    owner_z = owner // 4 % nz
    slot = (owner_z * nq + owner_q) * CAP + rank
    n_slots = n_owners * CAP
    to_slot = (iota((n_slots, n_points), 0) == slot).astype(F32).astype(BF16)
    local_hot = (iota((128, n_points), 0) == local + n_marks).astype(F32).astype(BF16)
    ids = dot(to_slot, local_hot, 1, 1)
    loads[0].wait()
    loads[1].wait()
    scores = dot(unit_rows(points[...]), unit_rows(marks[...]), 1, 1)
    rows = jnp.exp(scores * (0.5 / math.sqrt(depth)))
    rows = jnp.where(iota((n_points, 128), 1) < n_marks, rows, 0.0).astype(BF16)
    slots[...] = (dot(to_slot, rows) + ids).astype(BF16).reshape(nz, nq * CAP, 128)
    pl.semaphore_wait(barrier, len(everyone))

    p1 = [
        remote(piece_of(q), pieces.at[my_q], p1_send.at[q], p1_recv.at[my_q], device)
        for q, device in plane_peers
    ]
    rz = [
        remote(slots.at[z], rows_z.at[my_z], rz_send.at[z], rz_recv.at[my_z], device)
        for z, device in z_peers
    ]
    own = pltpu.make_async_copy(slots.at[my_z], rows_z.at[my_z], load_sem.at[4])
    for copy in rz + p1 + [own]:
        copy.start()

    source = index_ref[0]
    source_q = source // (nz * 4) * 4 + source % 4
    source_z = source // 4 % nz

    target = iota((n_slots, n_slots), 0)
    at_q, at_z, at_r = target // (nz * CAP), target // CAP % nz, target % CAP
    regroup = (iota((n_slots, n_slots), 1) == (at_z * nq + at_q) * CAP + at_r).astype(F32)
    regroup = regroup.astype(BF16)
    own.wait()
    for z, device in z_peers:
        remote(slots.at[z], rows_z.at[z], rz_send.at[z], rz_recv.at[z], device).wait_recv()
    grouped = dot(regroup, rows_z[...].reshape(n_slots, 128)).astype(BF16)
    regrouped[...] = grouped.reshape(nq, nz * CAP, 128)
    rq = [
        remote(regrouped.at[q], rows_q.at[my_q], rq_send.at[q], rq_recv.at[my_q], device)
        for q, device in plane_peers
    ]
    own = pltpu.make_async_copy(regrouped.at[my_q], rows_q.at[my_q], load_sem.at[4])
    for copy in rq + [own]:
        copy.start()

    loads[3].wait()
    for q, device in plane_peers:
        remote(piece_of(q), pieces.at[q], p1_send.at[q], p1_recv.at[q], device).wait_recv()
    planes[my_z] = pieces[source_q]
    p2 = [
        remote(planes.at[my_z], planes.at[my_z], p2_send.at[z], p2_recv.at[my_z], device)
        for z, device in z_peers
    ]
    for copy in p2:
        copy.start()

    own.wait()
    for q, device in plane_peers:
        remote(regrouped.at[q], rows_q.at[q], rq_send.at[q], rq_recv.at[q], device).wait_recv()
    received = rows_q[...].reshape(n_slots, 128)
    gram = dot(received, received, 0, 0)
    sums[my_l] = gram[n_marks:, :] * (OWNED * n_owners / (n_points * n_owners))
    s = [
        remote(sums.at[my_l], sums.at[my_l], s_send.at[l], s_recv.at[my_l], device)
        for l, device in l_peers
    ]
    for copy in s:
        copy.start()
    totals = dot(jnp.ones((8, n_slots), BF16), received)
    count_ref[...] = pltpu.roll(totals, 128 - n_marks, 1).astype(I32)

    for z, device in z_peers:
        remote(planes.at[z], planes.at[z], p2_send.at[z], p2_recv.at[z], device).wait_recv()
    panel[my_q] = planes[source_z]
    p3 = [
        remote(panel.at[my_q], panel.at[my_q], p3_send.at[q], p3_recv.at[my_q], device)
        for q, device in plane_peers
    ]
    for copy in p3:
        copy.start()

    for l, device in l_peers:
        remote(sums.at[l], sums.at[l], s_send.at[l], s_recv.at[l], device).wait_recv()
    factors = []
    for l in range(nl):
        whole = sums[l][:, :n_marks]
        high = whole.astype(BF16)
        factors.append(jnp.concatenate([high, (whole - high.astype(F32)).astype(BF16)], axis=0))
    for q, device in plane_peers:
        remote(panel.at[q], panel.at[q], p3_send.at[q], p3_recv.at[q], device).wait_recv()
    for column in range(4):
        both = dot(factors[0], panel[column])
        for l in range(1, nl):
            both = both + dot(factors[l], panel[l * 4 + column])
        out_ref[:, column * 128 : (column + 1) * 128] = both[:OWNED] + both[OWNED:]
    for copy in rz + p1 + rq + p2 + s + p3:
        copy.wait_send()


def solution(mesh):
    pts, nl = mesh.shape["pts"], mesh.shape["lmk"]
    nx = nl
    nz = pts // (nx * 4)
    nq = nx * 4

    def body(points, landmarks, panels, panel_index, assignment):
        n_points, depth = points.shape
        n_marks = landmarks.shape[0]
        columns = panels.shape[2]
        hbm = pl.BlockSpec(memory_space=pl.ANY)
        vmem = pl.BlockSpec(memory_space=pltpu.VMEM)
        dma = pltpu.SemaphoreType.DMA
        out, counts = pl.pallas_call(
            functools.partial(kernel, nx, nz, nl),
            out_shape=(
                jax.ShapeDtypeStruct((OWNED, columns), F32),
                jax.ShapeDtypeStruct((8, 128), I32),
            ),
            in_specs=[pl.BlockSpec(memory_space=pltpu.SMEM), hbm, hbm, hbm, hbm],
            out_specs=(vmem, vmem),
            scratch_shapes=[
                pltpu.VMEM((n_points, depth), BF16),
                pltpu.VMEM((128, depth), BF16),
                pltpu.VMEM((1, n_points), I32),
                pltpu.VMEM((nz, nq * CAP, 128), BF16),
                pltpu.VMEM((nz, nq * CAP, 128), BF16),
                pltpu.VMEM((nq, nz * CAP, 128), BF16),
                pltpu.VMEM((nq, nz * CAP, 128), BF16),
                pltpu.VMEM((nq, n_marks, 128), BF16),
                pltpu.VMEM((nz, n_marks, 128), BF16),
                pltpu.VMEM((nq, n_marks, 128), BF16),
                pltpu.VMEM((nl, OWNED, 128), F32),
                dma((5,)),
                dma((nz,)),
                dma((nz,)),
                dma((nq,)),
                dma((nq,)),
                dma((nq,)),
                dma((nq,)),
                dma((nz,)),
                dma((nz,)),
                dma((nq,)),
                dma((nq,)),
                dma((nl,)),
                dma((nl,)),
            ],
            compiler_params=pltpu.CompilerParams(collective_id=0, has_side_effects=True),
        )(panel_index, points, landmarks, panels, assignment.reshape(1, n_points))
        return out, counts[0, :OWNED]

    in_specs = (P("pts", None), P("lmk", None), P("pts", None, "lmk"), P(), P("pts"))
    out_specs = (P("pts", "lmk"), P("pts"))
    return jax.shard_map(body, mesh=mesh, in_specs=in_specs, out_specs=out_specs, check_vma=False)
```

```python
import functools
import math

import jax
import jax.numpy as jnp
from jax import lax
from jax.experimental import pallas as pl
from jax.experimental.pallas import tpu as pltpu
from jax.sharding import PartitionSpec as P

MESH = pl.DeviceIdType.MESH
CAP = 4
CHUNKS = 2
OWNED = 32
F32, BF16, I32 = jnp.float32, jnp.bfloat16, jnp.int32


def iota(shape, dim):
    return lax.broadcasted_iota(I32, shape, dim)


def dot(a, b, ca=1, cb=0):
    return lax.dot_general(a, b, (((ca,), (cb,)), ((), ())), preferred_element_type=F32)


def unit_rows(values):
    wide = values.astype(F32)
    scale = lax.rsqrt(jnp.mean(wide * wide, axis=1, keepdims=True) + 1e-06)
    return (wide * scale).astype(BF16)


def kernel(
    nx,
    nz,
    nl,
    index_hbm,
    points_hbm,
    marks_hbm,
    panel_hbm,
    assign_hbm,
    out_ref,
    count_ref,
    index_ref,
    points,
    marks,
    assign,
    mine,
    slots,
    rows_z,
    regrouped,
    rows_q,
    pieces,
    planes,
    panel,
    sums,
    load_sem,
    rz_send,
    rz_recv,
    rq_send,
    rq_recv,
    p1_send,
    p1_recv,
    p2_send,
    p2_recv,
    p3_send,
    p3_recv,
    s_send,
    s_recv,
):
    nq = nx * 4
    me, my_l = lax.axis_index("pts"), lax.axis_index("lmk")
    my_x, my_z, my_yc = me // (nz * 4), (me // 4) % nz, me % 4
    my_y, my_c = my_yc // 2, my_yc % 2
    my_q = my_x * 4 + my_yc
    n_marks, depth = marks_hbm.shape
    n_points = points_hbm.shape[0]

    plane_peers = []
    for dx in range(nx):
        for dy in range(2):
            for dc in range(2):
                if dx or dy or dc:
                    x = (my_x + dx) % nx
                    yc = (my_y + dy) % 2 * 2 + (my_c + dc) % 2
                    plane_peers.append((x * 4 + yc, ((x * nz + my_z) * 4 + yc, my_l)))
    z_peers = []
    for dz in range(1, nz):
        z = (my_z + dz) % nz
        z_peers.append((z, ((my_x * nz + z) * 4 + my_yc, my_l)))
    l_peers = []
    for dl in range(1, nl):
        l = (my_l + dl) % nl
        l_peers.append((l, (me, l)))

    step = n_marks // CHUNKS
    chunks = [pl.ds(k * step, step) for k in range(CHUNKS)]

    def chunk_at(ref, q, k):
        rows = pl.ds(pl.multiple_of(q // 4 * n_marks + k * step, step), step)
        return ref.at[rows, pl.ds(pl.multiple_of(q % 4 * 128, 128), 128)]

    loads = [
        pltpu.make_async_copy(points_hbm, points, load_sem.at[0]),
        pltpu.make_async_copy(marks_hbm, marks.at[pl.ds(0, n_marks)], load_sem.at[1]),
        pltpu.make_async_copy(assign_hbm, assign, load_sem.at[2]),
                pltpu.make_async_copy(panel_hbm.at[0], mine, load_sem.at[3]),
        pltpu.make_async_copy(index_hbm, index_ref, load_sem.at[5]),
    ]
    loads += [
        pltpu.make_async_copy(chunk_at(panel_hbm.at[0], my_q, k), pieces[k].at[my_q], load_sem.at[6 + k])
        for k in range(CHUNKS)
    ]
    barrier = pltpu.get_barrier_semaphore()
    everyone = z_peers + l_peers + plane_peers
    for _, device in everyone:
        pl.semaphore_signal(barrier, inc=1, device_id=device, device_id_type=MESH)
    for load in loads:
        load.start()

    def remote(src, dst, send, recv, device):
        return pltpu.make_async_remote_copy(
            src_ref=src,
            dst_ref=dst,
            send_sem=send,
            recv_sem=recv,
            device_id=device,
            device_id_type=MESH,
        )

    marks[n_marks:, :] = jnp.zeros((128 - n_marks, depth), BF16)
    loads[2].wait()
    assigned = assign[...]
    owner, local = assigned // OWNED, assigned % OWNED
    n_owners = nq * nz
    hits = iota((n_owners, n_points), 0) == owner
    earlier = (iota((n_points, n_points), 0) < iota((n_points, n_points), 1)).astype(F32)
    before = dot(hits.astype(BF16), earlier.astype(BF16))
    rank = jnp.sum(jnp.where(hits, before, 0.0), axis=0, keepdims=True).astype(I32)
    owner_q = owner // (nz * 4) * 4 + owner % 4
    owner_z = owner // 4 % nz
    slot = (owner_z * nq + owner_q) * CAP + rank
    n_slots = n_owners * CAP
    to_slot = (iota((n_slots, n_points), 0) == slot).astype(F32).astype(BF16)
    local_hot = (iota((128, n_points), 0) == local + n_marks).astype(F32).astype(BF16)
    ids = dot(to_slot, local_hot, 1, 1)
    loads[0].wait()
    loads[1].wait()
    scores = dot(unit_rows(points[...]), unit_rows(marks[...]), 1, 1)
    rows = jnp.exp(scores * (0.5 / math.sqrt(depth)))
    rows = jnp.where(iota((n_points, 128), 1) < n_marks, rows, 0.0).astype(BF16)
    slots[...] = (dot(to_slot, rows) + ids).astype(BF16).reshape(nz, nq * CAP, 128)
    pl.semaphore_wait(barrier, len(everyone))

    sent = []

    def start(copies):
        for copy in copies:
            copy.start()
        sent.extend(copies)

    def scatter_copies(k):
        out, back = [], []
        for q, device in plane_peers:
            src, send, recv, dst = chunk_at(mine, q, k), p1_send.at[k, q], p1_recv, pieces[k]
            out.append(remote(src, dst.at[my_q], send, recv.at[k, my_q], device))
            back.append(remote(src, dst.at[q], send, recv.at[k, q], device))
        return out, back

    def gather_copies(k):
        out, back = [], []
        for q, device in plane_peers:
            here, there, send = panel.at[my_q, chunks[k]], panel.at[q, chunks[k]], p3_send.at[k, q]
            out.append(remote(here, here, send, p3_recv.at[k, my_q], device))
            back.append(remote(there, there, send, p3_recv.at[k, q], device))
        return out, back

    def z_copies(k):
        out, back = [], []
        for z, device in z_peers:
            here, there, send = planes[k].at[my_z], planes[k].at[z], p2_send.at[k, z]
            out.append(remote(here, here, send, p2_recv.at[k, my_z], device))
            back.append(remote(there, there, send, p2_recv.at[k, z], device))
        return out, back

    def arrive(copies):
        for copy in copies:
            copy.wait_recv()

    rz, rz_back, rq, rq_back, s, s_back = [], [], [], [], [], []
    for z, device in z_peers:
        rz.append(remote(slots.at[z], rows_z.at[my_z], rz_send.at[z], rz_recv.at[my_z], device))
        rz_back.append(remote(slots.at[z], rows_z.at[z], rz_send.at[z], rz_recv.at[z], device))
    for q, device in plane_peers:
        rq.append(remote(regrouped.at[q], rows_q.at[my_q], rq_send.at[q], rq_recv.at[my_q], device))
        rq_back.append(remote(regrouped.at[q], rows_q.at[q], rq_send.at[q], rq_recv.at[q], device))
    for l, device in l_peers:
        s.append(remote(sums.at[my_l], sums.at[my_l], s_send.at[l], s_recv.at[my_l], device))
        s_back.append(remote(sums.at[l], sums.at[l], s_send.at[l], s_recv.at[l], device))
    own_z = pltpu.make_async_copy(slots.at[my_z], rows_z.at[my_z], load_sem.at[4])
    own_q = pltpu.make_async_copy(regrouped.at[my_q], rows_q.at[my_q], load_sem.at[4])
    p1 = [scatter_copies(k) for k in range(CHUNKS)]
    p2 = [z_copies(k) for k in range(CHUNKS)]
    p3 = [gather_copies(k) for k in range(CHUNKS)]

    def scatter(k):
        if k == 0:
            loads[3].wait()
        start(p1[k][0])

    def source():
        holder = index_ref[0, 0]
        return holder // (nz * 4) * 4 + holder % 4, holder // 4 % nz

    def along_z(k):
        if k == 0:
            loads[4].wait()
        loads[5 + k].wait()
        arrive(p1[k][1])
        planes[k][my_z] = pieces[k][source()[0]]
        start(p2[k][0])

    def gather(k):
        arrive(p2[k][1])
        panel[my_q, chunks[k]] = planes[k][source()[1]]
        start(p3[k][0])

    def rows_along_z():
        start(rz)
        own_z.start()

    def rows_in_plane():
        target = iota((n_slots, n_slots), 0)
        at_q, at_z, at_r = target // (nz * CAP), target // CAP % nz, target % CAP
        regroup = iota((n_slots, n_slots), 1) == (at_z * nq + at_q) * CAP + at_r
        regroup = regroup.astype(F32).astype(BF16)
        own_z.wait()
        arrive(rz_back)
        grouped = dot(regroup, rows_z[...].reshape(n_slots, 128)).astype(BF16)
        regrouped[...] = grouped.reshape(nq, nz * CAP, 128)
        start(rq)
        own_q.start()

    def sum_rows():
        own_q.wait()
        arrive(rq_back)
        received = rows_q[...].reshape(n_slots, 128)
        gram = dot(received, received, 0, 0)
        sums[my_l] = gram[n_marks:, :] * (OWNED * n_owners / (n_points * n_owners))
        start(s)
        totals = dot(jnp.ones((8, n_slots), BF16), received)
        count_ref[...] = pltpu.roll(totals, 128 - n_marks, 1)[:1, :OWNED].astype(I32)

    def finish():
        arrive(s_back)
        factors = []
        for l in range(nl):
            whole = sums[l][:, :n_marks]
            high = whole.astype(BF16)
            low = (whole - high.astype(F32)).astype(BF16)
            factors.append(jnp.concatenate([high, low], axis=0))
        for k in range(CHUNKS):
            arrive(p3[k][1])
        for column in range(4):
            both = dot(factors[0], panel[column])
            for l in range(1, nl):
                both = both + dot(factors[l], panel[l * 4 + column])
            out_ref[:, column * 128 : (column + 1) * 128] = both[:OWNED] + both[OWNED:]

    scatter(0)
    rows_along_z()
    for k in range(1, CHUNKS):
        scatter(k)
    along_z(0)
    rows_in_plane()
    for k in range(1, CHUNKS):
        along_z(k)
    gather(0)
    sum_rows()
    for k in range(1, CHUNKS):
        gather(k)
    finish()

    for copy in sent:
        copy.wait_send()


def write_out(total, count, out_hbm, count_hbm, sems):
    copies = [
        pltpu.make_async_copy(total, out_hbm, sems.at[0]),
        pltpu.make_async_copy(count, count_hbm, sems.at[1]),
    ]
    for copy in copies:
        copy.start()
    for copy in copies:
        copy.wait()


def solution(mesh):
    pts, nl = mesh.shape["pts"], mesh.shape["lmk"]
    nx = nl
    nz = pts // (nx * 4)
    nq = nx * 4

    def body(points, landmarks, panels, panel_index, assignment):
        n_points, depth = points.shape
        n_marks = landmarks.shape[0]
        columns = panels.shape[2]
        hbm = pl.BlockSpec(memory_space=pl.ANY)
        vmem = pl.BlockSpec(memory_space=pltpu.VMEM)
        dma = pltpu.SemaphoreType.DMA
        out, counts = pl.pallas_call(
            functools.partial(kernel, nx, nz, nl),
            out_shape=(
                pltpu.VMEM((OWNED, columns), F32),
                pltpu.VMEM((1, OWNED), I32),
            ),
            in_specs=[hbm] * 5,
            out_specs=(vmem, vmem),
            scratch_shapes=[
                pltpu.SMEM((1, 1), I32),
                pltpu.VMEM((n_points, depth), BF16),
                pltpu.VMEM((128, depth), BF16),
                pltpu.VMEM((1, n_points), I32),
                pltpu.VMEM((nl * n_marks, columns), BF16),
                pltpu.VMEM((nz, nq * CAP, 128), BF16),
                pltpu.VMEM((nz, nq * CAP, 128), BF16),
                pltpu.VMEM((nq, nz * CAP, 128), BF16),
                pltpu.VMEM((nq, nz * CAP, 128), BF16),
                [pltpu.VMEM((nq, n_marks // CHUNKS, 128), BF16)] * CHUNKS,
                [pltpu.VMEM((nz, n_marks // CHUNKS, 128), BF16)] * CHUNKS,
                pltpu.VMEM((nq, n_marks, 128), BF16),
                pltpu.VMEM((nl, OWNED, 128), F32),
                dma((6 + CHUNKS,)),
                dma((nz,)),
                dma((nz,)),
                dma((nq,)),
                dma((nq,)),
                dma((CHUNKS, nq)),
                dma((CHUNKS, nq)),
                dma((CHUNKS, nz)),
                dma((CHUNKS, nz)),
                dma((CHUNKS, nq)),
                dma((CHUNKS, nq)),
                dma((nl,)),
                dma((nl,)),
            ],
            compiler_params=pltpu.CompilerParams(collective_id=0, has_side_effects=True),
        )(panel_index.reshape(1, 1), points, landmarks, panels, assignment.reshape(1, n_points))
        out, counts = pl.pallas_call(
            write_out,
            out_shape=(
                jax.ShapeDtypeStruct((OWNED, columns), F32),
                jax.ShapeDtypeStruct((1, OWNED), I32),
            ),
            in_specs=[vmem, vmem],
            out_specs=(hbm, hbm),
            scratch_shapes=[dma((2,))],
        )(*(pltpu.with_memory_space_constraint(a, pltpu.VMEM) for a in (out, counts)))
        return out, counts.reshape(OWNED)

    in_specs = (P("pts", None), P("lmk", None), P("pts", None, "lmk"), P(), P("pts"))
    out_specs = (P("pts", "lmk"), P("pts"))
    return jax.shard_map(body, mesh=mesh, in_specs=in_specs, out_specs=out_specs, check_vma=False)
```

```python
import functools
import math

import jax
import jax.numpy as jnp
from jax import lax
from jax.experimental import pallas as pl
from jax.experimental.pallas import tpu as pltpu
from jax.sharding import PartitionSpec as P

MESH = pl.DeviceIdType.MESH
CAP = 4
CHUNKS = 3
OWNED = 32
F32, BF16, I32 = jnp.float32, jnp.bfloat16, jnp.int32


def iota(shape, dim):
    return lax.broadcasted_iota(I32, shape, dim)


def dot(a, b, ca=1, cb=0):
    return lax.dot_general(a, b, (((ca,), (cb,)), ((), ())), preferred_element_type=F32)


def unit_rows(values):
    wide = values.astype(F32)
    scale = lax.rsqrt(jnp.mean(wide * wide, axis=1, keepdims=True) + 1e-06)
    return (wide * scale).astype(BF16)


def kernel(
    nx,
    nz,
    nl,
    index_hbm,
    points_hbm,
    marks_hbm,
    panel_hbm,
    assign_hbm,
    out_ref,
    count_ref,
    index_ref,
    points,
    marks,
    assign,
    mine,
    halves,
    chosen,
    slots,
    rows_z,
    regrouped,
    rows_q,
    pieces,
    planes,
    panel,
    sums,
    load_sem,
    rz_send,
    rz_recv,
    rq_send,
    rq_recv,
    c1_send,
    c1_recv,
    p1_send,
    p1_recv,
    p2_send,
    p2_recv,
    p3_send,
    p3_recv,
    c3_send,
    c3_recv,
    s_send,
    s_recv,
    in_z,
    in_l,
):
    nq = nx * 4
    me, my_l = lax.axis_index("pts"), lax.axis_index("lmk")
    my_x, my_z, my_yc = me // (nz * 4), (me // 4) % nz, me % 4
    my_y, my_c = my_yc // 2, my_yc % 2
    my_q = my_x * 4 + my_yc
    n_marks, depth = marks_hbm.shape
    n_points = points_hbm.shape[0]

    plane_peers = []
    for dx in range(nx):
        for dy in range(2):
            for dc in range(2):
                if dx or dy or dc:
                    x = (my_x + dx) % nx
                    yc = (my_y + dy) % 2 * 2 + (my_c + dc) % 2
                    plane_peers.append((x * 4 + yc, ((x * nz + my_z) * 4 + yc, my_l)))
    other_c = 1 - my_c
    sibling = (me + other_c - my_c, my_l)
    my_xy = my_x * 2 + my_y
    xy_peers = []
    for dx in range(nx):
        for dy in range(2):
            if dx or dy:
                x, y = (my_x + dx) % nx, (my_y + dy) % 2
                xy_peers.append((x, y, ((x * nz + my_z) * 4 + y * 2 + my_c, my_l)))
    z_peers = []
    for dz in range(nz - 1, 0, -1):
        z = (my_z + dz) % nz
        z_peers.append((z, ((my_x * nz + z) * 4 + my_yc, my_l)))
    l_peers = []
    for dl in range(1, nl):
        l = (my_l + dl) % nl
        l_peers.append((l, (me, l)))

    step = n_marks // CHUNKS
    chunks = [pl.ds(k * step, step) for k in range(CHUNKS)]

    def half_of(ref, y, c, k):
        return ref.at[:, chunks[k], pl.ds(pl.multiple_of((y * 2 + c) * 128, 128), 128)]

    loads = [
        pltpu.make_async_copy(points_hbm, points, load_sem.at[0]),
        pltpu.make_async_copy(marks_hbm, marks.at[pl.ds(0, n_marks)], load_sem.at[1]),
        pltpu.make_async_copy(assign_hbm, assign, load_sem.at[2]),
                pltpu.make_async_copy(panel_hbm, mine, load_sem.at[3]),
        pltpu.make_async_copy(index_hbm, index_ref, load_sem.at[5]),
    ]
    loads += [
        pltpu.make_async_copy(
            half_of(panel_hbm, y, my_c, k), halves[k].at[my_c, y], load_sem.at[6 + 2 * k + y]
        )
        for k in range(CHUNKS)
        for y in range(2)
    ]
    barrier = pltpu.get_barrier_semaphore()

    def signal(semaphore, device):
        pl.semaphore_signal(semaphore, inc=1, device_id=device, device_id_type=MESH)

    for z, device in z_peers:
        pl.when(z > my_z)(functools.partial(signal, barrier, device))
    for _, device in plane_peers:
        signal(barrier, device)
    for l, device in l_peers:
        pl.when(l > my_l)(functools.partial(signal, barrier, device))
    for load in loads:
        load.start()

    def remote(src, dst, send, recv, device):
        return pltpu.make_async_remote_copy(
            src_ref=src,
            dst_ref=dst,
            send_sem=send,
            recv_sem=recv,
            device_id=device,
            device_id_type=MESH,
        )

    n_owners = nq * nz
    n_slots = n_owners * CAP
    made = {}

    def assign_slots():
        marks[n_marks:, :] = jnp.zeros((128 - n_marks, depth), BF16)
        loads[2].wait()
        assigned = assign[...]
        owner, local = assigned // OWNED, assigned % OWNED
        hits = iota((n_owners, n_points), 0) == owner
        earlier = (iota((n_points, n_points), 0) < iota((n_points, n_points), 1)).astype(F32)
        before = dot(hits.astype(BF16), earlier.astype(BF16))
        rank = jnp.sum(jnp.where(hits, before, 0.0), axis=0, keepdims=True).astype(I32)
        owner_q = owner // (nz * 4) * 4 + owner % 4
        owner_z = owner // 4 % nz
        slot = (owner_z * nq + owner_q) * CAP + rank
        to_slot = (iota((n_slots, n_points), 0) == slot).astype(F32).astype(BF16)
        local_hot = (iota((128, n_points), 0) == local + n_marks).astype(F32).astype(BF16)
        made["to_slot"], made["ids"] = to_slot, dot(to_slot, local_hot, 1, 1)

    def kernel_rows():
        loads[0].wait()
        loads[1].wait()
        scores = dot(unit_rows(points[...]), unit_rows(marks[...]), 1, 1)
        rows = jnp.exp(scores * (0.5 / math.sqrt(depth)))
        made["rows"] = jnp.where(iota((n_points, 128), 1) < n_marks, rows, 0.0).astype(BF16)

    def fill_slots():
        filled = dot(made["to_slot"], made["rows"]) + made["ids"]
        slots[...] = filled.astype(BF16).reshape(nz, nq * CAP, 128)

    def everyone_in():
        pl.semaphore_wait(barrier, len(plane_peers) + my_z + my_l)
        for z, device in z_peers:
            pl.when(z < my_z)(functools.partial(signal, in_z.at[my_z], device))
        for l, device in l_peers:
            pl.when(l < my_l)(functools.partial(signal, in_l.at[my_l], device))

    sent = []

    def start(copies):
        for copy in copies:
            copy.start()
        sent.extend(copies)

    def core_copies(k):
        out, back = [], []
        for y in range(2):
            src, send, recv = half_of(mine, y, other_c, k), c1_send.at[k, y], c1_recv.at[k, y]
            out.append(remote(src, halves[k].at[my_c, y], send, recv, sibling))
            back.append(remote(src, halves[k].at[other_c, y], send, recv, sibling))
        return out, back

    def scatter_copies(k):
        out, back = [], []
        for x, y, device in xy_peers:
            src, at, dst = chosen[k].at[y, x], x * 2 + y, pieces[k]
            out.append(remote(src, dst.at[my_xy], p1_send.at[k, at], p1_recv.at[k, my_xy], device))
            back.append(remote(src, dst.at[at], p1_send.at[k, at], p1_recv.at[k, at], device))
        return out, back

    def gather_copies(k):
        out, back = [], []
        here = panel.at[my_c, my_xy, chunks[k]]
        for x, y, device in xy_peers:
            at = x * 2 + y
            there = panel.at[my_c, at, chunks[k]]
            out.append(remote(here, here, p3_send.at[k, at], p3_recv.at[k, my_xy], device))
            back.append(remote(there, there, p3_send.at[k, at], p3_recv.at[k, at], device))
        return out, back

    def share_copies(k):
        here, there = panel.at[my_c, :, chunks[k]], panel.at[other_c, :, chunks[k]]
        out = remote(here, here, c3_send.at[k], c3_recv.at[k], sibling)
        return [out], [remote(there, there, c3_send.at[k], c3_recv.at[k], sibling)]

    def z_copies(k):
        out, back = [], []
        for z, device in z_peers:
            here, there, send = planes[k].at[my_z], planes[k].at[z], p2_send.at[k, z]
            out.append(remote(here, here, send, p2_recv.at[k, my_z], device))
            back.append(remote(there, there, send, p2_recv.at[k, z], device))
        return out, back

    def arrive(copies):
        for copy in copies:
            copy.wait_recv()

    rz, rz_back, rq, rq_back, s, s_back = [], [], [], [], [], []
    for z, device in z_peers:
        rz.append(remote(slots.at[z], rows_z.at[my_z], rz_send.at[z], rz_recv.at[my_z], device))
        rz_back.append(remote(slots.at[z], rows_z.at[z], rz_send.at[z], rz_recv.at[z], device))
    for q, device in plane_peers:
        rq.append(remote(regrouped.at[q], rows_q.at[my_q], rq_send.at[q], rq_recv.at[my_q], device))
        rq_back.append(remote(regrouped.at[q], rows_q.at[q], rq_send.at[q], rq_recv.at[q], device))
    for l, device in l_peers:
        s.append(remote(sums.at[my_l], sums.at[my_l], s_send.at[l], s_recv.at[my_l], device))
        s_back.append(remote(sums.at[l], sums.at[l], s_send.at[l], s_recv.at[l], device))
    own_z = pltpu.make_async_copy(slots.at[my_z], rows_z.at[my_z], load_sem.at[4])
    own_q = pltpu.make_async_copy(regrouped.at[my_q], rows_q.at[my_q], load_sem.at[4])
    c1 = [core_copies(k) for k in range(CHUNKS)]
    p1 = [scatter_copies(k) for k in range(CHUNKS)]
    p2 = [z_copies(k) for k in range(CHUNKS)]
    p3 = [gather_copies(k) for k in range(CHUNKS)]
    c3 = [share_copies(k) for k in range(CHUNKS)]

    def to_sibling(k):
        if k == 0:
            loads[3].wait()
        start(c1[k][0])

    def source():
        holder = index_ref[0, 0]
        yc = holder % 4
        return yc % 2, holder // (nz * 4) * 2 + yc // 2, holder // 4 % nz

    def scatter(k):
        if k == 0:
            loads[4].wait()
        for y in range(2):
            loads[5 + 2 * k + y].wait()
        arrive(c1[k][1])
        chosen[k][...] = halves[k][source()[0]]
        pieces[k][my_xy] = chosen[k][my_y, my_x]
        start(p1[k][0])

    def along_z(k):
        arrive(p1[k][1])
        planes[k][my_z] = pieces[k][source()[1]]
        start(p2[k][0])

    def gather(k):
        arrive(p2[k][1])
        panel[my_c, my_xy, chunks[k]] = planes[k][source()[2]]
        start(p3[k][0])

    def share(k):
        arrive(p3[k][1])
        start(c3[k][0])

    def rows_down():
        own_z.start()
        for (z, _), copy in zip(z_peers, rz):
            pl.when(z < my_z)(copy.start)

    def rows_up():
        for (z, _), copy in zip(z_peers, rz):

            @pl.when(z > my_z)
            def _():
                pl.semaphore_wait(in_z.at[z], 1)
                copy.start()

        sent.extend(rz)

    def rows_in_plane():
        target = iota((n_slots, n_slots), 0)
        at_q, at_z, at_r = target // (nz * CAP), target // CAP % nz, target % CAP
        regroup = iota((n_slots, n_slots), 1) == (at_z * nq + at_q) * CAP + at_r
        regroup = regroup.astype(F32).astype(BF16)
        own_z.wait()
        arrive(rz_back)
        grouped = dot(regroup, rows_z[...].reshape(n_slots, 128)).astype(BF16)
        regrouped[...] = grouped.reshape(nq, nz * CAP, 128)
        start(rq)
        own_q.start()

    def sum_rows():
        own_q.wait()
        arrive(rq_back)
        received = rows_q[...].reshape(n_slots, 128)
        gram = dot(received, received, 0, 0)
        sums[my_l] = gram[n_marks:, :] * (OWNED * n_owners / (n_points * n_owners))
        for l, _ in l_peers:
            pl.when(l > my_l)(functools.partial(pl.semaphore_wait, in_l.at[l], 1))
        start(s)
        totals = dot(jnp.ones((8, n_slots), BF16), received)
        count_ref[...] = pltpu.roll(totals, 128 - n_marks, 1)[:1, :OWNED].astype(I32)

    def finish():
        arrive(s_back)
        factors = []
        for l in range(nl):
            whole = sums[l][:, :n_marks]
            high = whole.astype(BF16)
            low = (whole - high.astype(F32)).astype(BF16)
            factors.append(jnp.concatenate([high, low], axis=0))
        for k in range(CHUNKS):
            arrive(c3[k][1])
        for column in range(4):
            both = dot(factors[0], panel[column % 2, column // 2])
            for l in range(1, nl):
                both = both + dot(factors[l], panel[column % 2, l * 2 + column // 2])
            out_ref[:, column * 128 : (column + 1) * 128] = both[:OWNED] + both[OWNED:]

    assign_slots()
    kernel_rows()
    fill_slots()
    everyone_in()
    for k in range(CHUNKS):
        to_sibling(k)
    rows_down()
    for k in range(CHUNKS):
        scatter(k)
    rows_up()
    for k in range(CHUNKS):
        along_z(k)
    rows_in_plane()
    for k in range(CHUNKS):
        gather(k)
    sum_rows()
    for k in range(CHUNKS):
        share(k)
    finish()
    for copy in sent:
        copy.wait_send()


def write_out(total, count, out_hbm, count_hbm, sems):
    copies = [
        pltpu.make_async_copy(total, out_hbm, sems.at[0]),
        pltpu.make_async_copy(count, count_hbm, sems.at[1]),
    ]
    for copy in copies:
        copy.start()
    for copy in copies:
        copy.wait()


def solution(mesh):
    pts, nl = mesh.shape["pts"], mesh.shape["lmk"]
    nx = nl
    nz = pts // (nx * 4)
    nq = nx * 4

    def body(points, landmarks, panels, panel_index, assignment):
        n_points, depth = points.shape
        n_marks = landmarks.shape[0]
        columns = panels.shape[2]
        step = n_marks // CHUNKS
        hbm = pl.BlockSpec(memory_space=pl.ANY)
        vmem = pl.BlockSpec(memory_space=pltpu.VMEM)
        dma = pltpu.SemaphoreType.DMA
        out, counts = pl.pallas_call(
            functools.partial(kernel, nx, nz, nl),
            out_shape=(
                pltpu.VMEM((OWNED, columns), F32),
                pltpu.VMEM((1, OWNED), I32),
            ),
            in_specs=[hbm] * 5,
            out_specs=(vmem, vmem),
            scratch_shapes=[
                pltpu.SMEM((1, 1), I32),
                pltpu.VMEM((n_points, depth), BF16),
                pltpu.VMEM((128, depth), BF16),
                pltpu.VMEM((1, n_points), I32),
                pltpu.VMEM((nl, n_marks, columns), BF16),
                [pltpu.VMEM((2, 2, nx, step, 128), BF16)] * CHUNKS,
                [pltpu.VMEM((2, nx, step, 128), BF16)] * CHUNKS,
                pltpu.VMEM((nz, nq * CAP, 128), BF16),
                pltpu.VMEM((nz, nq * CAP, 128), BF16),
                pltpu.VMEM((nq, nz * CAP, 128), BF16),
                pltpu.VMEM((nq, nz * CAP, 128), BF16),
                [pltpu.VMEM((nx * 2, step, 128), BF16)] * CHUNKS,
                [pltpu.VMEM((nz, step, 128), BF16)] * CHUNKS,
                pltpu.VMEM((2, nx * 2, n_marks, 128), BF16),
                pltpu.VMEM((nl, OWNED, 128), F32),
                dma((6 + 2 * CHUNKS,)),
                dma((nz,)),
                dma((nz,)),
                dma((nq,)),
                dma((nq,)),
                dma((CHUNKS, 2)),
                dma((CHUNKS, 2)),
                dma((CHUNKS, nx * 2)),
                dma((CHUNKS, nx * 2)),
                dma((CHUNKS, nz)),
                dma((CHUNKS, nz)),
                dma((CHUNKS, nx * 2)),
                dma((CHUNKS, nx * 2)),
                dma((CHUNKS,)),
                dma((CHUNKS,)),
                dma((nl,)),
                dma((nl,)),
                pltpu.SemaphoreType.REGULAR((nz,)),
                pltpu.SemaphoreType.REGULAR((nl,)),
            ],
            compiler_params=pltpu.CompilerParams(collective_id=0, has_side_effects=True),
        )(panel_index.reshape(1, 1), points, landmarks, panels.reshape(nl, n_marks, columns), assignment.reshape(1, n_points))
        out, counts = pl.pallas_call(
            write_out,
            out_shape=(
                jax.ShapeDtypeStruct((OWNED, columns), F32),
                jax.ShapeDtypeStruct((1, OWNED), I32),
            ),
            in_specs=[vmem, vmem],
            out_specs=(hbm, hbm),
            scratch_shapes=[dma((2,))],
        )(*(pltpu.with_memory_space_constraint(a, pltpu.VMEM) for a in (out, counts)))
        return out, counts.reshape(OWNED)

    in_specs = (P("pts", None), P("lmk", None), P("pts", None, "lmk"), P(), P("pts"))
    out_specs = (P("pts", "lmk"), P("pts"))
    return jax.shard_map(body, mesh=mesh, in_specs=in_specs, out_specs=out_specs, check_vma=False)
```

```python
import functools
import math

import jax
import jax.numpy as jnp
from jax import lax
from jax.experimental import pallas as pl
from jax.experimental.pallas import tpu as pltpu
from jax.sharding import PartitionSpec as P

MESH = pl.DeviceIdType.MESH
CAP = 4
CHUNKS = 3
OWNED = 32
F32, BF16, I32 = jnp.float32, jnp.bfloat16, jnp.int32


def iota(shape, dim):
    return lax.broadcasted_iota(I32, shape, dim)


def dot(a, b, ca=1, cb=0):
    return lax.dot_general(a, b, (((ca,), (cb,)), ((), ())), preferred_element_type=F32)


def unit_rows(values):
    wide = values.astype(F32)
    scale = lax.rsqrt(jnp.mean(wide * wide, axis=1, keepdims=True) + 1e-06)
    return (wide * scale).astype(BF16)


def kernel(
    nx,
    nz,
    nl,
    index_hbm,
    points_hbm,
    marks_hbm,
    panel_hbm,
    assign_hbm,
    out_ref,
    count_ref,
    index_ref,
    points,
    marks,
    assign,
    mine,
    halves,
    chosen,
    slots,
    rows_z,
    regrouped,
    rows_q,
    pieces,
    planes,
    panel,
    sums,
    load_sem,
    rz_send,
    rz_recv,
    rq_send,
    rq_recv,
    c1_send,
    c1_recv,
    p1_send,
    p1_recv,
    p2_send,
    p2_recv,
    p3_send,
    p3_recv,
    c3_send,
    c3_recv,
    s_send,
    s_recv,
    in_z,
    in_l,
):
    nq = nx * 4
    me, my_l = lax.axis_index("pts"), lax.axis_index("lmk")
    my_x, my_z, my_yc = me // (nz * 4), (me // 4) % nz, me % 4
    my_y, my_c = my_yc // 2, my_yc % 2
    my_q = my_x * 4 + my_yc
    n_marks, depth = marks_hbm.shape
    n_points = points_hbm.shape[0]

    plane_peers = []
    for dx in range(nx):
        for dy in range(2):
            for dc in range(2):
                if dx or dy or dc:
                    x = (my_x + dx) % nx
                    yc = (my_y + dy) % 2 * 2 + (my_c + dc) % 2
                    plane_peers.append((x * 4 + yc, ((x * nz + my_z) * 4 + yc, my_l)))
    other_c = 1 - my_c
    sibling = (me + other_c - my_c, my_l)
    my_xy = my_x * 2 + my_y
    xy_peers = []
    for dx in range(nx):
        for dy in range(2):
            if dx or dy:
                x, y = (my_x + dx) % nx, (my_y + dy) % 2
                xy_peers.append((x, y, ((x * nz + my_z) * 4 + y * 2 + my_c, my_l)))
    z_peers = []
    for dz in range(nz - 1, 0, -1):
        z = (my_z + dz) % nz
        z_peers.append((z, ((my_x * nz + z) * 4 + my_yc, my_l)))
    l_peers = []
    for dl in range(1, nl):
        l = (my_l + dl) % nl
        l_peers.append((l, (me, l)))

    step = n_marks // CHUNKS
    chunks = [pl.ds(k * step, step) for k in range(CHUNKS)]

    def half_of(ref, y, c, k):
        return ref.at[:, chunks[k], pl.ds(pl.multiple_of((y * 2 + c) * 128, 128), 128)]

    loads = [
        pltpu.make_async_copy(points_hbm, points, load_sem.at[0]),
        pltpu.make_async_copy(marks_hbm, marks.at[pl.ds(0, n_marks)], load_sem.at[1]),
        pltpu.make_async_copy(assign_hbm, assign, load_sem.at[2]),
                pltpu.make_async_copy(panel_hbm, mine, load_sem.at[3]),
        pltpu.make_async_copy(index_hbm, index_ref, load_sem.at[5]),
    ]
    loads += [
        pltpu.make_async_copy(
            half_of(panel_hbm, y, my_c, k), halves[k].at[my_c, y], load_sem.at[6 + 2 * k + y]
        )
        for k in range(CHUNKS)
        for y in range(2)
    ]
    barrier = pltpu.get_barrier_semaphore()

    def signal(semaphore, device):
        pl.semaphore_signal(semaphore, inc=1, device_id=device, device_id_type=MESH)

    for load in loads[:3]:
        load.start()
    for _, device in plane_peers[::-1]:
        signal(barrier, device)
    for z, device in z_peers:
        pl.when(z > my_z)(functools.partial(signal, barrier, device))
    for l, device in l_peers:
        pl.when(l > my_l)(functools.partial(signal, barrier, device))
    for load in loads[3:]:
        load.start()

    def remote(src, dst, send, recv, device):
        return pltpu.make_async_remote_copy(
            src_ref=src,
            dst_ref=dst,
            send_sem=send,
            recv_sem=recv,
            device_id=device,
            device_id_type=MESH,
        )

    n_owners = nq * nz
    n_slots = n_owners * CAP
    made = {}

    def assign_slots():
        marks[n_marks:, :] = jnp.zeros((128 - n_marks, depth), BF16)
        loads[2].wait()
        assigned = assign[...]
        owner, local = assigned // OWNED, assigned % OWNED
        hits = iota((n_owners, n_points), 0) == owner
        earlier = (iota((n_points, n_points), 0) < iota((n_points, n_points), 1)).astype(F32)
        before = dot(hits.astype(BF16), earlier.astype(BF16))
        rank = jnp.sum(jnp.where(hits, before, 0.0), axis=0, keepdims=True).astype(I32)
        owner_q = owner // (nz * 4) * 4 + owner % 4
        owner_z = owner // 4 % nz
        slot = (owner_z * nq + owner_q) * CAP + rank
        to_slot = (iota((n_slots, n_points), 0) == slot).astype(F32).astype(BF16)
        local_hot = (iota((128, n_points), 0) == local + n_marks).astype(F32).astype(BF16)
        made["to_slot"], made["ids"] = to_slot, dot(to_slot, local_hot, 1, 1)

    def kernel_rows():
        loads[0].wait()
        loads[1].wait()
        scores = dot(unit_rows(points[...]), unit_rows(marks[...]), 1, 1)
        rows = jnp.exp(scores * (0.5 / math.sqrt(depth)))
        made["rows"] = jnp.where(iota((n_points, 128), 1) < n_marks, rows, 0.0).astype(BF16)

    def fill_slots():
        filled = dot(made["to_slot"], made["rows"]) + made["ids"]
        slots[...] = filled.astype(BF16).reshape(nz, nq * CAP, 128)

    def everyone_in():
        pl.semaphore_wait(barrier, len(plane_peers) + my_z + my_l)
        for z, device in z_peers:
            pl.when(z < my_z)(functools.partial(signal, in_z.at[my_z], device))
        for l, device in l_peers:
            pl.when(l < my_l)(functools.partial(signal, in_l.at[my_l], device))

    sent = []

    def start(copies):
        for copy in copies:
            copy.start()
        sent.extend(copies)

    def core_copies(k):
        out, back = [], []
        for y in range(2):
            src, send, recv = half_of(mine, y, other_c, k), c1_send.at[k, y], c1_recv.at[k, y]
            out.append(remote(src, halves[k].at[my_c, y], send, recv, sibling))
            back.append(remote(src, halves[k].at[other_c, y], send, recv, sibling))
        return out, back

    def scatter_copies(k):
        out, back = [], []
        for x, y, device in xy_peers:
            src, at, dst = chosen[k].at[y, x], x * 2 + y, pieces[k]
            out.append(remote(src, dst.at[my_xy], p1_send.at[k, at], p1_recv.at[k, my_xy], device))
            back.append(remote(src, dst.at[at], p1_send.at[k, at], p1_recv.at[k, at], device))
        return out, back

    def gather_copies(k):
        out, back = [], []
        here = panel.at[my_c, my_xy, chunks[k]]
        for x, y, device in xy_peers:
            at = x * 2 + y
            there = panel.at[my_c, at, chunks[k]]
            out.append(remote(here, here, p3_send.at[k, at], p3_recv.at[k, my_xy], device))
            back.append(remote(there, there, p3_send.at[k, at], p3_recv.at[k, at], device))
        return out, back

    def share_copies(k):
        here, there = panel.at[my_c, :, chunks[k]], panel.at[other_c, :, chunks[k]]
        out = remote(here, here, c3_send.at[k], c3_recv.at[k], sibling)
        return [out], [remote(there, there, c3_send.at[k], c3_recv.at[k], sibling)]

    def z_copies(k):
        out, back = [], []
        for z, device in z_peers:
            here, there, send = planes[k].at[my_z], planes[k].at[z], p2_send.at[k, z]
            out.append(remote(here, here, send, p2_recv.at[k, my_z], device))
            back.append(remote(there, there, send, p2_recv.at[k, z], device))
        return out, back

    def arrive(copies):
        for copy in copies:
            copy.wait_recv()

    rz, rz_back, rq, rq_back, s, s_back = [], [], [], [], [], []
    for z, device in z_peers:
        rz.append(remote(slots.at[z], rows_z.at[my_z], rz_send.at[z], rz_recv.at[my_z], device))
        rz_back.append(remote(slots.at[z], rows_z.at[z], rz_send.at[z], rz_recv.at[z], device))
    for q, device in plane_peers:
        rq.append(remote(regrouped.at[q], rows_q.at[my_q], rq_send.at[q], rq_recv.at[my_q], device))
        rq_back.append(remote(regrouped.at[q], rows_q.at[q], rq_send.at[q], rq_recv.at[q], device))
    for l, device in l_peers:
        s.append(remote(sums.at[my_l], sums.at[my_l], s_send.at[l], s_recv.at[my_l], device))
        s_back.append(remote(sums.at[l], sums.at[l], s_send.at[l], s_recv.at[l], device))
    own_z = pltpu.make_async_copy(slots.at[my_z], rows_z.at[my_z], load_sem.at[4])
    own_q = pltpu.make_async_copy(regrouped.at[my_q], rows_q.at[my_q], load_sem.at[4])
    c1 = [core_copies(k) for k in range(CHUNKS)]
    p1 = [scatter_copies(k) for k in range(CHUNKS)]
    p2 = [z_copies(k) for k in range(CHUNKS)]
    p3 = [gather_copies(k) for k in range(CHUNKS)]
    c3 = [share_copies(k) for k in range(CHUNKS)]

    def to_sibling(k):
        if k == 0:
            loads[3].wait()
        start(c1[k][0])

    def source():
        holder = index_ref[0, 0]
        yc = holder % 4
        return yc % 2, holder // (nz * 4) * 2 + yc // 2, holder // 4 % nz

    def scatter(k):
        if k == 0:
            loads[4].wait()
        for y in range(2):
            loads[5 + 2 * k + y].wait()
        arrive(c1[k][1])
        chosen[k][...] = halves[k][source()[0]]
        pieces[k][my_xy] = chosen[k][my_y, my_x]
        start(p1[k][0])

    def along_z(k):
        arrive(p1[k][1])
        planes[k][my_z] = pieces[k][source()[1]]
        start(p2[k][0])

    def gather(k):
        arrive(p2[k][1])
        panel[my_c, my_xy, chunks[k]] = planes[k][source()[2]]
        start(p3[k][0])

    def share(k):
        arrive(p3[k][1])
        start(c3[k][0])

    def rows_down():
        own_z.start()
        for (z, _), copy in zip(z_peers, rz):
            pl.when(z < my_z)(copy.start)

    def rows_up():
        for (z, _), copy in zip(z_peers, rz):

            @pl.when(z > my_z)
            def _():
                pl.semaphore_wait(in_z.at[z], 1)
                copy.start()

        sent.extend(rz)

    def order_rows():
        target = iota((n_slots, n_slots), 0)
        at_q, at_z, at_r = target // (nz * CAP), target // CAP % nz, target % CAP
        regroup = iota((n_slots, n_slots), 1) == (at_z * nq + at_q) * CAP + at_r
        regroup = regroup.astype(F32).astype(BF16)
        made["regroup"] = regroup

    def rows_in_plane():
        own_z.wait()
        arrive(rz_back)
        grouped = dot(made["regroup"], rows_z[...].reshape(n_slots, 128)).astype(BF16)
        regrouped[...] = grouped.reshape(nq, nz * CAP, 128)
        start(rq)
        own_q.start()

    def sum_rows():
        own_q.wait()
        arrive(rq_back)
        received = rows_q[...].reshape(n_slots, 128)
        gram = dot(received, received, 0, 0)
        sums[my_l] = gram[n_marks:, :] * (OWNED * n_owners / (n_points * n_owners))
        for l, _ in l_peers:
            pl.when(l > my_l)(functools.partial(pl.semaphore_wait, in_l.at[l], 1))
        start(s)
        totals = dot(jnp.ones((8, n_slots), BF16), received)
        count_ref[...] = pltpu.roll(totals, 128 - n_marks, 1)[:1, :OWNED].astype(I32)

    def finish():
        arrive(s_back)
        factors = []
        for l in range(nl):
            whole = sums[l][:, :n_marks]
            high = whole.astype(BF16)
            low = (whole - high.astype(F32)).astype(BF16)
            factors.append(jnp.concatenate([high, low], axis=0))
        for k in range(CHUNKS):
            arrive(c3[k][1])
        for column in range(4):
            both = dot(factors[0], panel[column % 2, column // 2])
            for l in range(1, nl):
                both = both + dot(factors[l], panel[column % 2, l * 2 + column // 2])
            out_ref[:, column * 128 : (column + 1) * 128] = both[:OWNED] + both[OWNED:]

    assign_slots()
    kernel_rows()
    everyone_in()
    for k in range(CHUNKS):
        to_sibling(k)
    fill_slots()
    rows_down()
    for k in range(CHUNKS):
        scatter(k)
    rows_up()
    order_rows()
    for k in range(CHUNKS):
        along_z(k)
    rows_in_plane()
    gather(0)
    gather(1)
    sum_rows()
    gather(2)
    for k in range(CHUNKS):
        share(k)
    finish()
    for copy in sent:
        copy.wait_send()


def write_out(total, count, out_hbm, count_hbm, sems):
    copies = [
        pltpu.make_async_copy(total, out_hbm, sems.at[0]),
        pltpu.make_async_copy(count, count_hbm, sems.at[1]),
    ]
    for copy in copies:
        copy.start()
    for copy in copies:
        copy.wait()


def solution(mesh):
    pts, nl = mesh.shape["pts"], mesh.shape["lmk"]
    nx = nl
    nz = pts // (nx * 4)
    nq = nx * 4

    def body(points, landmarks, panels, panel_index, assignment):
        n_points, depth = points.shape
        n_marks = landmarks.shape[0]
        columns = panels.shape[2]
        step = n_marks // CHUNKS
        hbm = pl.BlockSpec(memory_space=pl.ANY)
        vmem = pl.BlockSpec(memory_space=pltpu.VMEM)
        dma = pltpu.SemaphoreType.DMA
        out, counts = pl.pallas_call(
            functools.partial(kernel, nx, nz, nl),
            out_shape=(
                pltpu.VMEM((OWNED, columns), F32),
                pltpu.VMEM((1, OWNED), I32),
            ),
            in_specs=[hbm] * 5,
            out_specs=(vmem, vmem),
            scratch_shapes=[
                pltpu.SMEM((1, 1), I32),
                pltpu.VMEM((n_points, depth), BF16),
                pltpu.VMEM((128, depth), BF16),
                pltpu.VMEM((1, n_points), I32),
                pltpu.VMEM((nl, n_marks, columns), BF16),
                [pltpu.VMEM((2, 2, nx, step, 128), BF16)] * CHUNKS,
                [pltpu.VMEM((2, nx, step, 128), BF16)] * CHUNKS,
                pltpu.VMEM((nz, nq * CAP, 128), BF16),
                pltpu.VMEM((nz, nq * CAP, 128), BF16),
                pltpu.VMEM((nq, nz * CAP, 128), BF16),
                pltpu.VMEM((nq, nz * CAP, 128), BF16),
                [pltpu.VMEM((nx * 2, step, 128), BF16)] * CHUNKS,
                [pltpu.VMEM((nz, step, 128), BF16)] * CHUNKS,
                pltpu.VMEM((2, nx * 2, n_marks, 128), BF16),
                pltpu.VMEM((nl, OWNED, 128), F32),
                dma((6 + 2 * CHUNKS,)),
                dma((nz,)),
                dma((nz,)),
                dma((nq,)),
                dma((nq,)),
                dma((CHUNKS, 2)),
                dma((CHUNKS, 2)),
                dma((CHUNKS, nx * 2)),
                dma((CHUNKS, nx * 2)),
                dma((CHUNKS, nz)),
                dma((CHUNKS, nz)),
                dma((CHUNKS, nx * 2)),
                dma((CHUNKS, nx * 2)),
                dma((CHUNKS,)),
                dma((CHUNKS,)),
                dma((nl,)),
                dma((nl,)),
                pltpu.SemaphoreType.REGULAR((nz,)),
                pltpu.SemaphoreType.REGULAR((nl,)),
            ],
            compiler_params=pltpu.CompilerParams(collective_id=0, has_side_effects=True),
        )(panel_index.reshape(1, 1), points, landmarks, panels.reshape(nl, n_marks, columns), assignment.reshape(1, n_points))
        out, counts = pl.pallas_call(
            write_out,
            out_shape=(
                jax.ShapeDtypeStruct((OWNED, columns), F32),
                jax.ShapeDtypeStruct((1, OWNED), I32),
            ),
            in_specs=[vmem, vmem],
            out_specs=(hbm, hbm),
            scratch_shapes=[dma((2,))],
        )(*(pltpu.with_memory_space_constraint(a, pltpu.VMEM) for a in (out, counts)))
        return out, counts.reshape(OWNED)

    in_specs = (P("pts", None), P("lmk", None), P("pts", None, "lmk"), P(), P("pts"))
    out_specs = (P("pts", "lmk"), P("pts"))
    return jax.shard_map(body, mesh=mesh, in_specs=in_specs, out_specs=out_specs, check_vma=False)
```

```python
import functools
import math

import jax
import jax.numpy as jnp
from jax import lax
from jax.experimental import pallas as pl
from jax.experimental.pallas import tpu as pltpu
from jax.sharding import PartitionSpec as P

MESH = pl.DeviceIdType.MESH
CAP = 4
CHUNKS = 3
OWNED = 32
F32, BF16, I32 = jnp.float32, jnp.bfloat16, jnp.int32


def iota(shape, dim):
    return lax.broadcasted_iota(I32, shape, dim)


def dot(a, b, ca=1, cb=0):
    return lax.dot_general(a, b, (((ca,), (cb,)), ((), ())), preferred_element_type=F32)


def unit_rows(values):
    wide = values.astype(F32)
    scale = lax.rsqrt(jnp.mean(wide * wide, axis=1, keepdims=True) + 1e-06)
    return (wide * scale).astype(BF16)


def kernel(
    nx,
    nz,
    nl,
    index_hbm,
    points_hbm,
    marks_hbm,
    panel_hbm,
    assign_hbm,
    out_ref,
    count_ref,
    index_ref,
    points,
    marks,
    assign,
    mine,
    halves,
    chosen,
    slots,
    rows_z,
    regrouped,
    rows_q,
    pieces,
    planes,
    panel,
    sums,
    load_sem,
    rz_send,
    rz_recv,
    rq_send,
    rq_recv,
    c1_send,
    c1_recv,
    p1_send,
    p1_recv,
    p2_send,
    p2_recv,
    p3_send,
    p3_recv,
    c3_send,
    c3_recv,
    s_send,
    s_recv,
    in_z,
    in_l,
):
    nq = nx * 4
    me, my_l = lax.axis_index("pts"), lax.axis_index("lmk")
    my_x, my_z, my_yc = me // (nz * 4), (me // 4) % nz, me % 4
    my_y, my_c = my_yc // 2, my_yc % 2
    my_q = my_x * 4 + my_yc
    n_marks, depth = marks_hbm.shape
    n_points = points_hbm.shape[0]

    plane_peers = []
    far_x = sorted(range(nx), key=lambda d: -min(d, nx - d))
    for dx in far_x:
        for dy in (1, 0):
            for dc in (1, 0):
                if dx or dy or dc:
                    x = (my_x + dx) % nx
                    yc = (my_y + dy) % 2 * 2 + (my_c + dc) % 2
                    plane_peers.append((x * 4 + yc, ((x * nz + my_z) * 4 + yc, my_l)))
    other_c = 1 - my_c
    sibling = (me + other_c - my_c, my_l)
    my_xy = my_x * 2 + my_y
    xy_peers = []
    for dx in far_x:
        for dy in (1, 0):
            if dx or dy:
                x, y = (my_x + dx) % nx, (my_y + dy) % 2
                xy_peers.append((x, y, ((x * nz + my_z) * 4 + y * 2 + my_c, my_l)))
    z_peers = []
    for dz in range(nz - 1, 0, -1):
        z = (my_z + dz) % nz
        z_peers.append((z, ((my_x * nz + z) * 4 + my_yc, my_l)))
    l_peers = []
    for dl in sorted(range(1, nl), key=lambda d: -min(d, nl - d)):
        l = (my_l + dl) % nl
        l_peers.append((l, (me, l)))

    step = n_marks // CHUNKS
    chunks = [pl.ds(k * step, step) for k in range(CHUNKS)]

    def half_of(ref, y, c, k):
        return ref.at[:, chunks[k], pl.ds(pl.multiple_of((y * 2 + c) * 128, 128), 128)]

    loads = [
        pltpu.make_async_copy(points_hbm, points, load_sem.at[0]),
        pltpu.make_async_copy(marks_hbm, marks.at[pl.ds(0, n_marks)], load_sem.at[1]),
        pltpu.make_async_copy(assign_hbm, assign, load_sem.at[2]),
                pltpu.make_async_copy(panel_hbm, mine, load_sem.at[3]),
        pltpu.make_async_copy(index_hbm, index_ref, load_sem.at[5]),
    ]
    loads += [
        pltpu.make_async_copy(
            half_of(panel_hbm, y, my_c, k), halves[k].at[my_c, y], load_sem.at[6 + 2 * k + y]
        )
        for k in range(CHUNKS)
        for y in range(2)
    ]
    barrier = pltpu.get_barrier_semaphore()

    def signal(semaphore, device):
        pl.semaphore_signal(semaphore, inc=1, device_id=device, device_id_type=MESH)

    for load in loads[:3]:
        load.start()
    for _, device in plane_peers:
        signal(barrier, device)
    for z, device in z_peers:
        pl.when(z > my_z)(functools.partial(signal, barrier, device))
    for l, device in l_peers:
        pl.when(l > my_l)(functools.partial(signal, barrier, device))
    for load in loads[3:]:
        load.start()

    def remote(src, dst, send, recv, device):
        return pltpu.make_async_remote_copy(
            src_ref=src,
            dst_ref=dst,
            send_sem=send,
            recv_sem=recv,
            device_id=device,
            device_id_type=MESH,
        )

    n_owners = nq * nz
    n_slots = n_owners * CAP
    made = {}

    def assign_slots():
        marks[n_marks:, :] = jnp.zeros((128 - n_marks, depth), BF16)
        loads[2].wait()
        assigned = assign[...]
        owner, local = assigned // OWNED, assigned % OWNED
        hits = iota((n_owners, n_points), 0) == owner
        earlier = (iota((n_points, n_points), 0) < iota((n_points, n_points), 1)).astype(F32)
        before = dot(hits.astype(BF16), earlier.astype(BF16))
        rank = jnp.sum(jnp.where(hits, before, 0.0), axis=0, keepdims=True).astype(I32)
        owner_q = owner // (nz * 4) * 4 + owner % 4
        owner_z = owner // 4 % nz
        slot = (owner_z * nq + owner_q) * CAP + rank
        to_slot = (iota((n_slots, n_points), 0) == slot).astype(F32).astype(BF16)
        local_hot = (iota((128, n_points), 0) == local + n_marks).astype(F32).astype(BF16)
        made["to_slot"], made["ids"] = to_slot, dot(to_slot, local_hot, 1, 1)

    def kernel_rows():
        loads[0].wait()
        loads[1].wait()
        scores = dot(unit_rows(points[...]), unit_rows(marks[...]), 1, 1)
        rows = jnp.exp(scores * (0.5 / math.sqrt(depth)))
        made["rows"] = jnp.where(iota((n_points, 128), 1) < n_marks, rows, 0.0).astype(BF16)

    def fill_slots():
        filled = dot(made["to_slot"], made["rows"]) + made["ids"]
        slots[...] = filled.astype(BF16).reshape(nz, nq * CAP, 128)

    def everyone_in():
        pl.semaphore_wait(barrier, len(plane_peers) + my_z + my_l)
        for z, device in z_peers:
            pl.when(z < my_z)(functools.partial(signal, in_z.at[my_z], device))
        for l, device in l_peers:
            pl.when(l < my_l)(functools.partial(signal, in_l.at[my_l], device))

    sent = []

    def start(copies):
        for copy in copies:
            copy.start()
        sent.extend(copies)

    def core_copies(k):
        out, back = [], []
        for y in range(2):
            src, send, recv = half_of(mine, y, other_c, k), c1_send.at[k, y], c1_recv.at[k, y]
            out.append(remote(src, halves[k].at[my_c, y], send, recv, sibling))
            back.append(remote(src, halves[k].at[other_c, y], send, recv, sibling))
        return out, back

    def scatter_copies(k):
        out, back = [], []
        for x, y, device in xy_peers:
            src, at, dst = chosen[k].at[y, x], x * 2 + y, pieces[k]
            out.append(remote(src, dst.at[my_xy], p1_send.at[k, at], p1_recv.at[k, my_xy], device))
            back.append(remote(src, dst.at[at], p1_send.at[k, at], p1_recv.at[k, at], device))
        return out, back

    def gather_copies(k):
        out, back = [], []
        here = panel.at[my_c, my_xy, chunks[k]]
        for x, y, device in xy_peers:
            at = x * 2 + y
            there = panel.at[my_c, at, chunks[k]]
            out.append(remote(here, here, p3_send.at[k, at], p3_recv.at[k, my_xy], device))
            back.append(remote(there, there, p3_send.at[k, at], p3_recv.at[k, at], device))
        return out, back

    def share_copies(k):
        here, there = panel.at[my_c, :, chunks[k]], panel.at[other_c, :, chunks[k]]
        out = remote(here, here, c3_send.at[k], c3_recv.at[k], sibling)
        return [out], [remote(there, there, c3_send.at[k], c3_recv.at[k], sibling)]

    def z_copies(k):
        out, back = [], []
        for z, device in z_peers:
            here, there, send = planes[k].at[my_z], planes[k].at[z], p2_send.at[k, z]
            out.append(remote(here, here, send, p2_recv.at[k, my_z], device))
            back.append(remote(there, there, send, p2_recv.at[k, z], device))
        return out, back

    def arrive(copies):
        for copy in copies:
            copy.wait_recv()

    rz, rz_back, rq, rq_back, s, s_back = [], [], [], [], [], []
    for z, device in z_peers:
        rz.append(remote(slots.at[z], rows_z.at[my_z], rz_send.at[z], rz_recv.at[my_z], device))
        rz_back.append(remote(slots.at[z], rows_z.at[z], rz_send.at[z], rz_recv.at[z], device))
    for q, device in plane_peers:
        rq.append(remote(regrouped.at[q], rows_q.at[my_q], rq_send.at[q], rq_recv.at[my_q], device))
        rq_back.append(remote(regrouped.at[q], rows_q.at[q], rq_send.at[q], rq_recv.at[q], device))
    for l, device in l_peers:
        s.append(remote(sums.at[my_l], sums.at[my_l], s_send.at[l], s_recv.at[my_l], device))
        s_back.append(remote(sums.at[l], sums.at[l], s_send.at[l], s_recv.at[l], device))
    own_z = pltpu.make_async_copy(slots.at[my_z], rows_z.at[my_z], load_sem.at[4])
    own_q = pltpu.make_async_copy(regrouped.at[my_q], rows_q.at[my_q], load_sem.at[4])
    c1 = [core_copies(k) for k in range(CHUNKS)]
    p1 = [scatter_copies(k) for k in range(CHUNKS)]
    p2 = [z_copies(k) for k in range(CHUNKS)]
    p3 = [gather_copies(k) for k in range(CHUNKS)]
    c3 = [share_copies(k) for k in range(CHUNKS)]

    def to_sibling(k):
        if k == 0:
            loads[3].wait()
        start(c1[k][0])

    def source():
        holder = index_ref[0, 0]
        yc = holder % 4
        return yc % 2, holder // (nz * 4) * 2 + yc // 2, holder // 4 % nz

    def scatter(k):
        if k == 0:
            loads[4].wait()
        for y in range(2):
            loads[5 + 2 * k + y].wait()
        arrive(c1[k][1])
        chosen[k][...] = halves[k][source()[0]]
        pieces[k][my_xy] = chosen[k][my_y, my_x]
        start(p1[k][0])

    def along_z(k):
        arrive(p1[k][1])
        planes[k][my_z] = pieces[k][source()[1]]
        start(p2[k][0])

    def gather(k):
        arrive(p2[k][1])
        panel[my_c, my_xy, chunks[k]] = planes[k][source()[2]]
        start(p3[k][0])

    def share(k):
        arrive(p3[k][1])
        start(c3[k][0])

    def rows_down():
        own_z.start()
        for (z, _), copy in zip(z_peers, rz):
            pl.when(z < my_z)(copy.start)

    def rows_up():
        for (z, _), copy in zip(z_peers, rz):

            @pl.when(z > my_z)
            def _():
                pl.semaphore_wait(in_z.at[z], 1)
                copy.start()

        sent.extend(rz)

    def order_rows():
        target = iota((n_slots, n_slots), 0)
        at_q, at_z, at_r = target // (nz * CAP), target // CAP % nz, target % CAP
        regroup = iota((n_slots, n_slots), 1) == (at_z * nq + at_q) * CAP + at_r
        regroup = regroup.astype(F32).astype(BF16)
        made["regroup"] = regroup

    def rows_in_plane():
        own_z.wait()
        arrive(rz_back)
        grouped = dot(made["regroup"], rows_z[...].reshape(n_slots, 128)).astype(BF16)
        regrouped[...] = grouped.reshape(nq, nz * CAP, 128)
        start(rq)
        own_q.start()

    def sum_rows():
        own_q.wait()
        arrive(rq_back)
        received = rows_q[...].reshape(n_slots, 128)
        gram = dot(received, received, 0, 0)
        sums[my_l] = gram[n_marks:, :] * (OWNED * n_owners / (n_points * n_owners))
        for l, _ in l_peers:
            pl.when(l > my_l)(functools.partial(pl.semaphore_wait, in_l.at[l], 1))
        start(s)
        totals = dot(jnp.ones((8, n_slots), BF16), received)
        count_ref[...] = pltpu.roll(totals, 128 - n_marks, 1)[:1, :OWNED].astype(I32)

    def finish():
        arrive(s_back)
        factors = []
        for l in range(nl):
            whole = sums[l][:, :n_marks]
            high = whole.astype(BF16)
            low = (whole - high.astype(F32)).astype(BF16)
            factors.append(jnp.concatenate([high, low], axis=0))
        for k in range(CHUNKS):
            arrive(c3[k][1])
        for column in range(4):
            both = dot(factors[0], panel[column % 2, column // 2])
            for l in range(1, nl):
                both = both + dot(factors[l], panel[column % 2, l * 2 + column // 2])
            out_ref[:, column * 128 : (column + 1) * 128] = both[:OWNED] + both[OWNED:]

    assign_slots()
    kernel_rows()
    everyone_in()
    for k in range(CHUNKS):
        to_sibling(k)
    fill_slots()
    rows_down()
    for k in range(CHUNKS):
        scatter(k)
    rows_up()
    order_rows()
    for k in range(CHUNKS):
        along_z(k)
    rows_in_plane()
    gather(0)
    gather(1)
    sum_rows()
    gather(2)
    for k in range(CHUNKS):
        share(k)
    finish()
    for copy in sent:
        copy.wait_send()


def write_out(total, count, out_hbm, count_hbm, sems):
    copies = [
        pltpu.make_async_copy(total, out_hbm, sems.at[0]),
        pltpu.make_async_copy(count, count_hbm, sems.at[1]),
    ]
    for copy in copies:
        copy.start()
    for copy in copies:
        copy.wait()


def solution(mesh):
    pts, nl = mesh.shape["pts"], mesh.shape["lmk"]
    nx = nl
    nz = pts // (nx * 4)
    nq = nx * 4

    def body(points, landmarks, panels, panel_index, assignment):
        n_points, depth = points.shape
        n_marks = landmarks.shape[0]
        columns = panels.shape[2]
        step = n_marks // CHUNKS
        hbm = pl.BlockSpec(memory_space=pl.ANY)
        vmem = pl.BlockSpec(memory_space=pltpu.VMEM)
        dma = pltpu.SemaphoreType.DMA
        out, counts = pl.pallas_call(
            functools.partial(kernel, nx, nz, nl),
            out_shape=(
                pltpu.VMEM((OWNED, columns), F32),
                pltpu.VMEM((1, OWNED), I32),
            ),
            in_specs=[hbm] * 5,
            out_specs=(vmem, vmem),
            scratch_shapes=[
                pltpu.SMEM((1, 1), I32),
                pltpu.VMEM((n_points, depth), BF16),
                pltpu.VMEM((128, depth), BF16),
                pltpu.VMEM((1, n_points), I32),
                pltpu.VMEM((nl, n_marks, columns), BF16),
                [pltpu.VMEM((2, 2, nx, step, 128), BF16)] * CHUNKS,
                [pltpu.VMEM((2, nx, step, 128), BF16)] * CHUNKS,
                pltpu.VMEM((nz, nq * CAP, 128), BF16),
                pltpu.VMEM((nz, nq * CAP, 128), BF16),
                pltpu.VMEM((nq, nz * CAP, 128), BF16),
                pltpu.VMEM((nq, nz * CAP, 128), BF16),
                [pltpu.VMEM((nx * 2, step, 128), BF16)] * CHUNKS,
                [pltpu.VMEM((nz, step, 128), BF16)] * CHUNKS,
                pltpu.VMEM((2, nx * 2, n_marks, 128), BF16),
                pltpu.VMEM((nl, OWNED, 128), F32),
                dma((6 + 2 * CHUNKS,)),
                dma((nz,)),
                dma((nz,)),
                dma((nq,)),
                dma((nq,)),
                dma((CHUNKS, 2)),
                dma((CHUNKS, 2)),
                dma((CHUNKS, nx * 2)),
                dma((CHUNKS, nx * 2)),
                dma((CHUNKS, nz)),
                dma((CHUNKS, nz)),
                dma((CHUNKS, nx * 2)),
                dma((CHUNKS, nx * 2)),
                dma((CHUNKS,)),
                dma((CHUNKS,)),
                dma((nl,)),
                dma((nl,)),
                pltpu.SemaphoreType.REGULAR((nz,)),
                pltpu.SemaphoreType.REGULAR((nl,)),
            ],
            compiler_params=pltpu.CompilerParams(collective_id=0, has_side_effects=True),
        )(panel_index.reshape(1, 1), points, landmarks, panels.reshape(nl, n_marks, columns), assignment.reshape(1, n_points))
        out, counts = pl.pallas_call(
            write_out,
            out_shape=(
                jax.ShapeDtypeStruct((OWNED, columns), F32),
                jax.ShapeDtypeStruct((1, OWNED), I32),
            ),
            in_specs=[vmem, vmem],
            out_specs=(hbm, hbm),
            scratch_shapes=[dma((2,))],
        )(*(pltpu.with_memory_space_constraint(a, pltpu.VMEM) for a in (out, counts)))
        return out, counts.reshape(OWNED)

    in_specs = (P("pts", None), P("lmk", None), P("pts", None, "lmk"), P(), P("pts"))
    out_specs = (P("pts", "lmk"), P("pts"))
    return jax.shard_map(body, mesh=mesh, in_specs=in_specs, out_specs=out_specs, check_vma=False)
```

```python
import functools
import math

import jax
import jax.numpy as jnp
from jax import lax
from jax.experimental import pallas as pl
from jax.experimental.pallas import tpu as pltpu
from jax.sharding import PartitionSpec as P

MESH = pl.DeviceIdType.MESH
CAP = 4
CHUNKS = 3
OWNED = 32
F32, BF16, I32 = jnp.float32, jnp.bfloat16, jnp.int32


def iota(shape, dim):
    return lax.broadcasted_iota(I32, shape, dim)


def dot(a, b, ca=1, cb=0):
    return lax.dot_general(a, b, (((ca,), (cb,)), ((), ())), preferred_element_type=F32)


def unit_rows(values):
    wide = values.astype(F32)
    scale = lax.rsqrt(jnp.mean(wide * wide, axis=1, keepdims=True) + 1e-06)
    return (wide * scale).astype(BF16)


def kernel(
    nx,
    nz,
    nl,
    index_hbm,
    points_hbm,
    marks_hbm,
    panel_hbm,
    assign_hbm,
    out_ref,
    count_ref,
    index_ref,
    points,
    marks,
    assign,
    mine,
    halves,
    chosen,
    slots,
    rows_z,
    regrouped,
    rows_q,
    pieces,
    planes,
    panel,
    sums,
    load_sem,
    rz_send,
    rz_recv,
    rq_send,
    rq_recv,
    c1_send,
    c1_recv,
    p1_send,
    p1_recv,
    p2_send,
    p2_recv,
    p3_send,
    p3_recv,
    c3_send,
    c3_recv,
    s_send,
    s_recv,
    in_z,
    in_l,
):
    nq = nx * 4
    me, my_l = lax.axis_index("pts"), lax.axis_index("lmk")
    my_x, my_z, my_yc = me // (nz * 4), (me // 4) % nz, me % 4
    my_y, my_c = my_yc // 2, my_yc % 2
    my_q = my_x * 4 + my_yc
    n_marks, depth = marks_hbm.shape
    n_points = points_hbm.shape[0]

    plane_peers = []
    far_x = sorted(range(nx), key=lambda d: -min(d, nx - d))
    for dx in far_x:
        for dy in (1, 0):
            for dc in (1, 0):
                if dx or dy or dc:
                    x = (my_x + dx) % nx
                    yc = (my_y + dy) % 2 * 2 + (my_c + dc) % 2
                    plane_peers.append((x * 4 + yc, ((x * nz + my_z) * 4 + yc, my_l)))
    other_c = 1 - my_c
    sibling = (me + other_c - my_c, my_l)
    my_xy = my_x * 2 + my_y
    xy_peers = []
    for dx in far_x:
        for dy in (1, 0):
            if dx or dy:
                x, y = (my_x + dx) % nx, (my_y + dy) % 2
                xy_peers.append((x, y, ((x * nz + my_z) * 4 + y * 2 + my_c, my_l)))
    z_peers = []
    for dz in range(nz - 1, 0, -1):
        z = (my_z + dz) % nz
        z_peers.append((z, ((my_x * nz + z) * 4 + my_yc, my_l)))
    l_peers = []
    for dl in sorted(range(1, nl), key=lambda d: -min(d, nl - d)):
        l = (my_l + dl) % nl
        l_peers.append((l, (me, l)))

    step = n_marks // CHUNKS
    chunks = [pl.ds(k * step, step) for k in range(CHUNKS)]

    def half_of(ref, y, c, k):
        return ref.at[:, chunks[k], pl.ds(pl.multiple_of((y * 2 + c) * 128, 128), 128)]

    loads = [
        pltpu.make_async_copy(points_hbm, points, load_sem.at[0]),
        pltpu.make_async_copy(marks_hbm, marks.at[pl.ds(0, n_marks)], load_sem.at[1]),
        pltpu.make_async_copy(assign_hbm, assign, load_sem.at[2]),
                pltpu.make_async_copy(panel_hbm, mine, load_sem.at[3]),
        pltpu.make_async_copy(index_hbm, index_ref, load_sem.at[5]),
    ]
    loads += [
        pltpu.make_async_copy(
            half_of(panel_hbm, y, my_c, k), halves[k].at[my_c, y], load_sem.at[6 + 2 * k + y]
        )
        for k in range(CHUNKS)
        for y in range(2)
    ]
    barrier = pltpu.get_barrier_semaphore()

    def signal(semaphore, device):
        pl.semaphore_signal(semaphore, inc=1, device_id=device, device_id_type=MESH)

    for load in loads[:3]:
        load.start()
    for _, device in plane_peers:
        signal(barrier, device)
    for z, device in z_peers:
        pl.when(z > my_z)(functools.partial(signal, barrier, device))
    for l, device in l_peers:
        pl.when(l > my_l)(functools.partial(signal, barrier, device))
    for load in loads[3:]:
        load.start()

    def remote(src, dst, send, recv, device):
        return pltpu.make_async_remote_copy(
            src_ref=src,
            dst_ref=dst,
            send_sem=send,
            recv_sem=recv,
            device_id=device,
            device_id_type=MESH,
        )

    n_owners = nq * nz
    n_slots = n_owners * CAP
    made = {}

    def assign_slots():
        marks[n_marks:, :] = jnp.zeros((128 - n_marks, depth), BF16)
        loads[2].wait()
        assigned = assign[...]
        owner, local = assigned // OWNED, assigned % OWNED
        hits = iota((n_owners, n_points), 0) == owner
        earlier = (iota((n_points, n_points), 0) < iota((n_points, n_points), 1)).astype(F32)
        before = dot(hits.astype(BF16), earlier.astype(BF16))
        rank = jnp.sum(jnp.where(hits, before, 0.0), axis=0, keepdims=True).astype(I32)
        owner_q = owner // (nz * 4) * 4 + owner % 4
        owner_z = owner // 4 % nz
        slot = (owner_z * nq + owner_q) * CAP + rank
        to_slot = (iota((n_slots, n_points), 0) == slot).astype(F32).astype(BF16)
        local_hot = (iota((128, n_points), 0) == local + n_marks).astype(F32).astype(BF16)
        made["to_slot"], made["ids"] = to_slot, dot(to_slot, local_hot, 1, 1)

    def kernel_rows():
        loads[0].wait()
        loads[1].wait()
        scores = dot(unit_rows(points[...]), unit_rows(marks[...]), 1, 1)
        rows = jnp.exp(scores * (0.5 / math.sqrt(depth)))
        made["rows"] = jnp.where(iota((n_points, 128), 1) < n_marks, rows, 0.0).astype(BF16)

    def fill_slots():
        filled = dot(made["to_slot"], made["rows"]) + made["ids"]
        slots[...] = filled.astype(BF16).reshape(nz, nq * CAP, 128)

    def everyone_in():
        pl.semaphore_wait(barrier, len(plane_peers) + my_z + my_l)
        for z, device in z_peers:
            pl.when(z < my_z)(functools.partial(signal, in_z.at[my_z], device))
        for l, device in l_peers:
            pl.when(l < my_l)(functools.partial(signal, in_l.at[my_l], device))

    sent = []

    def start(copies):
        for copy in copies:
            copy.start()
        sent.extend(copies)

    def core_copies(k):
        out, back = [], []
        for y in range(2):
            src, send, recv = half_of(mine, y, other_c, k), c1_send.at[k, y], c1_recv.at[k, y]
            out.append(remote(src, halves[k].at[my_c, y], send, recv, sibling))
            back.append(remote(src, halves[k].at[other_c, y], send, recv, sibling))
        return out, back

    def scatter_copies(k):
        out, back = [], []
        for x, y, device in xy_peers:
            src, at, dst = chosen[k].at[y, x], x * 2 + y, pieces[k]
            out.append(remote(src, dst.at[my_xy], p1_send.at[k, at], p1_recv.at[k, my_xy], device))
            back.append(remote(src, dst.at[at], p1_send.at[k, at], p1_recv.at[k, at], device))
        return out, back

    def gather_copies(k):
        out, back = [], []
        here = panel.at[my_c, my_xy, chunks[k]]
        for x, y, device in xy_peers:
            at = x * 2 + y
            there = panel.at[my_c, at, chunks[k]]
            out.append(remote(here, here, p3_send.at[k, at], p3_recv.at[k, my_xy], device))
            back.append(remote(there, there, p3_send.at[k, at], p3_recv.at[k, at], device))
        return out, back

    def share_copies(k):
        here, there = panel.at[my_c, :, chunks[k]], panel.at[other_c, :, chunks[k]]
        out = remote(here, here, c3_send.at[k], c3_recv.at[k], sibling)
        return [out], [remote(there, there, c3_send.at[k], c3_recv.at[k], sibling)]

    def z_copies(k):
        out, back = [], []
        for z, device in z_peers:
            here, there, send = planes[k].at[my_z], planes[k].at[z], p2_send.at[k, z]
            out.append(remote(here, here, send, p2_recv.at[k, my_z], device))
            back.append(remote(there, there, send, p2_recv.at[k, z], device))
        return out, back

    def arrive(copies):
        for copy in copies:
            copy.wait_recv()

    rz, rz_back, rq, rq_back, s, s_back = [], [], [], [], [], []
    for z, device in z_peers:
        rz.append(remote(slots.at[z], rows_z.at[my_z], rz_send.at[z], rz_recv.at[my_z], device))
        rz_back.append(remote(slots.at[z], rows_z.at[z], rz_send.at[z], rz_recv.at[z], device))
    for q, device in plane_peers:
        rq.append(remote(regrouped.at[q], rows_q.at[my_q], rq_send.at[q], rq_recv.at[my_q], device))
        rq_back.append(remote(regrouped.at[q], rows_q.at[q], rq_send.at[q], rq_recv.at[q], device))
    for l, device in l_peers:
        s.append(remote(sums.at[my_l], sums.at[my_l], s_send.at[l], s_recv.at[my_l], device))
        s_back.append(remote(sums.at[l], sums.at[l], s_send.at[l], s_recv.at[l], device))
    own_z = pltpu.make_async_copy(slots.at[my_z], rows_z.at[my_z], load_sem.at[4])
    own_q = pltpu.make_async_copy(regrouped.at[my_q], rows_q.at[my_q], load_sem.at[4])
    c1 = [core_copies(k) for k in range(CHUNKS)]
    p1 = [scatter_copies(k) for k in range(CHUNKS)]
    p2 = [z_copies(k) for k in range(CHUNKS)]
    p3 = [gather_copies(k) for k in range(CHUNKS)]
    c3 = [share_copies(k) for k in range(CHUNKS)]

    def to_sibling(k):
        if k == 0:
            loads[3].wait()
        start(c1[k][0])

    def source():
        holder = index_ref[0, 0]
        yc = holder % 4
        return yc % 2, holder // (nz * 4) * 2 + yc // 2, holder // 4 % nz

    def scatter(k):
        if k == 0:
            loads[4].wait()
        for y in range(2):
            loads[5 + 2 * k + y].wait()
        arrive(c1[k][1])
        chosen[k][...] = halves[k][source()[0]]
        pieces[k][my_xy] = chosen[k][my_y, my_x]
        start(p1[k][0])

    def along_z(k):
        arrive(p1[k][1])
        planes[k][my_z] = pieces[k][source()[1]]
        start(p2[k][0])

    def gather(k):
        arrive(p2[k][1])
        panel[my_c, my_xy, chunks[k]] = planes[k][source()[2]]
        start(p3[k][0])

    def share(k):
        arrive(p3[k][1])
        start(c3[k][0])

    def rows_down():
        own_z.start()
        for (z, _), copy in zip(z_peers, rz):
            pl.when(z < my_z)(copy.start)

    def rows_up():
        for (z, _), copy in zip(z_peers, rz):

            @pl.when(z > my_z)
            def _():
                pl.semaphore_wait(in_z.at[z], 1)
                copy.start()

        sent.extend(rz)

    def order_rows():
        target = iota((n_slots, n_slots), 0)
        at_q, at_z, at_r = target // (nz * CAP), target // CAP % nz, target % CAP
        regroup = iota((n_slots, n_slots), 1) == (at_z * nq + at_q) * CAP + at_r
        regroup = regroup.astype(F32).astype(BF16)
        made["regroup"] = regroup

    def rows_in_plane():
        own_z.wait()
        arrive(rz_back)
        grouped = dot(made["regroup"], rows_z[...].reshape(n_slots, 128)).astype(BF16)
        regrouped[...] = grouped.reshape(nq, nz * CAP, 128)
        start(rq)
        own_q.start()

    def sum_rows():
        own_q.wait()
        arrive(rq_back)
        received = rows_q[...].reshape(n_slots, 128)
        gram = dot(received, received, 0, 0)
        sums[my_l] = gram[n_marks:, :] * (OWNED * n_owners / (n_points * n_owners))
        for l, _ in l_peers:
            pl.when(l > my_l)(functools.partial(pl.semaphore_wait, in_l.at[l], 1))
        start(s)
        totals = dot(jnp.ones((8, n_slots), BF16), received)
        count_ref[...] = pltpu.roll(totals, 128 - n_marks, 1)[:1, :OWNED].astype(I32)

    def finish():
        arrive(s_back)
        factors = []
        for l in range(nl):
            whole = sums[l][:, :n_marks]
            high = whole.astype(BF16)
            low = (whole - high.astype(F32)).astype(BF16)
            factors.append(jnp.concatenate([high, low], axis=0))
        for c in (my_c, other_c):
            for y in range(2):
                both = dot(factors[0], panel[c, y])
                for l in range(1, nl):
                    both = both + dot(factors[l], panel[c, l * 2 + y])
                column = pl.multiple_of((y * 2 + c) * 128, 128)
                out_ref[:, pl.ds(column, 128)] = both[:OWNED] + both[OWNED:]
            if c is my_c:
                for k in range(CHUNKS):
                    arrive(c3[k][1])

    assign_slots()
    kernel_rows()
    fill_slots()
    everyone_in()
    rows_down()
    for k in range(CHUNKS):
        to_sibling(k)
    for k in range(CHUNKS):
        scatter(k)
    rows_up()
    order_rows()
    for k in range(CHUNKS):
        along_z(k)
    rows_in_plane()
    gather(0)
    gather(1)
    sum_rows()
    gather(2)
    for k in range(CHUNKS):
        share(k)
    finish()
    for copy in sent:
        copy.wait_send()


def write_out(total, count, out_hbm, count_hbm, sems):
    copies = [
        pltpu.make_async_copy(total, out_hbm, sems.at[0]),
        pltpu.make_async_copy(count, count_hbm, sems.at[1]),
    ]
    for copy in copies:
        copy.start()
    for copy in copies:
        copy.wait()


def solution(mesh):
    pts, nl = mesh.shape["pts"], mesh.shape["lmk"]
    nx = nl
    nz = pts // (nx * 4)
    nq = nx * 4

    def body(points, landmarks, panels, panel_index, assignment):
        n_points, depth = points.shape
        n_marks = landmarks.shape[0]
        columns = panels.shape[2]
        step = n_marks // CHUNKS
        hbm = pl.BlockSpec(memory_space=pl.ANY)
        vmem = pl.BlockSpec(memory_space=pltpu.VMEM)
        dma = pltpu.SemaphoreType.DMA
        out, counts = pl.pallas_call(
            functools.partial(kernel, nx, nz, nl),
            out_shape=(
                pltpu.VMEM((OWNED, columns), F32),
                pltpu.VMEM((1, OWNED), I32),
            ),
            in_specs=[hbm] * 5,
            out_specs=(vmem, vmem),
            scratch_shapes=[
                pltpu.SMEM((1, 1), I32),
                pltpu.VMEM((n_points, depth), BF16),
                pltpu.VMEM((128, depth), BF16),
                pltpu.VMEM((1, n_points), I32),
                pltpu.VMEM((nl, n_marks, columns), BF16),
                [pltpu.VMEM((2, 2, nx, step, 128), BF16)] * CHUNKS,
                [pltpu.VMEM((2, nx, step, 128), BF16)] * CHUNKS,
                pltpu.VMEM((nz, nq * CAP, 128), BF16),
                pltpu.VMEM((nz, nq * CAP, 128), BF16),
                pltpu.VMEM((nq, nz * CAP, 128), BF16),
                pltpu.VMEM((nq, nz * CAP, 128), BF16),
                [pltpu.VMEM((nx * 2, step, 128), BF16)] * CHUNKS,
                [pltpu.VMEM((nz, step, 128), BF16)] * CHUNKS,
                pltpu.VMEM((2, nx * 2, n_marks, 128), BF16),
                pltpu.VMEM((nl, OWNED, 128), F32),
                dma((6 + 2 * CHUNKS,)),
                dma((nz,)),
                dma((nz,)),
                dma((nq,)),
                dma((nq,)),
                dma((CHUNKS, 2)),
                dma((CHUNKS, 2)),
                dma((CHUNKS, nx * 2)),
                dma((CHUNKS, nx * 2)),
                dma((CHUNKS, nz)),
                dma((CHUNKS, nz)),
                dma((CHUNKS, nx * 2)),
                dma((CHUNKS, nx * 2)),
                dma((CHUNKS,)),
                dma((CHUNKS,)),
                dma((nl,)),
                dma((nl,)),
                pltpu.SemaphoreType.REGULAR((nz,)),
                pltpu.SemaphoreType.REGULAR((nl,)),
            ],
            compiler_params=pltpu.CompilerParams(collective_id=0, has_side_effects=True),
        )(panel_index.reshape(1, 1), points, landmarks, panels.reshape(nl, n_marks, columns), assignment.reshape(1, n_points))
        out, counts = pl.pallas_call(
            write_out,
            out_shape=(
                jax.ShapeDtypeStruct((OWNED, columns), F32),
                jax.ShapeDtypeStruct((1, OWNED), I32),
            ),
            in_specs=[vmem, vmem],
            out_specs=(hbm, hbm),
            scratch_shapes=[dma((2,))],
        )(*(pltpu.with_memory_space_constraint(a, pltpu.VMEM) for a in (out, counts)))
        return out, counts.reshape(OWNED)

    in_specs = (P("pts", None), P("lmk", None), P("pts", None, "lmk"), P(), P("pts"))
    out_specs = (P("pts", "lmk"), P("pts"))
    return jax.shard_map(body, mesh=mesh, in_specs=in_specs, out_specs=out_specs, check_vma=False)
```

```python
import functools
import math

import jax
import jax.numpy as jnp
from jax import lax
from jax.experimental import pallas as pl
from jax.experimental.pallas import tpu as pltpu
from jax.sharding import PartitionSpec as P

MESH = pl.DeviceIdType.MESH
CAP = 4
CHUNKS = 3
OWNED = 32
F32, BF16, I32 = jnp.float32, jnp.bfloat16, jnp.int32


def iota(shape, dim):
    return lax.broadcasted_iota(I32, shape, dim)


def dot(a, b, ca=1, cb=0):
    return lax.dot_general(a, b, (((ca,), (cb,)), ((), ())), preferred_element_type=F32)


def unit_rows(values):
    wide = values.astype(F32)
    scale = lax.rsqrt(jnp.mean(wide * wide, axis=1, keepdims=True) + 1e-06)
    return (wide * scale).astype(BF16)


def kernel(
    nx,
    nz,
    nl,
    index_hbm,
    points_hbm,
    marks_hbm,
    panel_hbm,
    assign_hbm,
    out_ref,
    count_ref,
    index_ref,
    points,
    marks,
    assign,
    mine,
    halves,
    chosen,
    slots,
    rows_z,
    regrouped,
    rows_q,
    pieces,
    planes,
    panel,
    sums,
    load_sem,
    rz_send,
    rz_recv,
    rq_send,
    rq_recv,
    c1_send,
    c1_recv,
    p1_send,
    p1_recv,
    p2_send,
    p2_recv,
    p3_send,
    p3_recv,
    c3_send,
    c3_recv,
    s_send,
    s_recv,
    in_z,
    in_l,
):
    nq = nx * 4
    me, my_l = lax.axis_index("pts"), lax.axis_index("lmk")
    my_x, my_z, my_yc = me // (nz * 4), (me // 4) % nz, me % 4
    my_y, my_c = my_yc // 2, my_yc % 2
    my_q = my_x * 4 + my_yc
    n_marks, depth = marks_hbm.shape
    n_points = points_hbm.shape[0]

    plane_peers = []
    far_x = sorted(range(nx), key=lambda d: -min(d, nx - d))
    for dx in far_x:
        for dy in (1, 0):
            for dc in (1, 0):
                if dx or dy or dc:
                    x = (my_x + dx) % nx
                    yc = (my_y + dy) % 2 * 2 + (my_c + dc) % 2
                    plane_peers.append((x * 4 + yc, ((x * nz + my_z) * 4 + yc, my_l)))
    other_c = 1 - my_c
    sibling = (me + other_c - my_c, my_l)
    my_xy = my_x * 2 + my_y
    xy_peers = []
    for dx in far_x:
        for dy in (1, 0):
            if dx or dy:
                x, y = (my_x + dx) % nx, (my_y + dy) % 2
                xy_peers.append((x, y, ((x * nz + my_z) * 4 + y * 2 + my_c, my_l)))
    z_peers = []
    for dz in range(nz - 1, 0, -1):
        z = (my_z + dz) % nz
        z_peers.append((z, ((my_x * nz + z) * 4 + my_yc, my_l)))
    l_peers = []
    for dl in sorted(range(1, nl), key=lambda d: -min(d, nl - d)):
        l = (my_l + dl) % nl
        l_peers.append((l, (me, l)))

    step = n_marks // CHUNKS
    chunks = [pl.ds(k * step, step) for k in range(CHUNKS)]

    def half_of(ref, y, c, k):
        return ref.at[:, chunks[k], pl.ds(pl.multiple_of((y * 2 + c) * 128, 128), 128)]

    loads = [
        pltpu.make_async_copy(points_hbm, points, load_sem.at[0]),
        pltpu.make_async_copy(marks_hbm, marks.at[pl.ds(0, n_marks)], load_sem.at[1]),
        pltpu.make_async_copy(assign_hbm, assign, load_sem.at[2]),
                pltpu.make_async_copy(panel_hbm, mine, load_sem.at[3]),
        pltpu.make_async_copy(index_hbm, index_ref, load_sem.at[5]),
    ]
    loads += [
        pltpu.make_async_copy(
            half_of(panel_hbm, y, my_c, k), halves[k].at[my_c, y], load_sem.at[6 + 2 * k + y]
        )
        for k in range(CHUNKS)
        for y in range(2)
    ]
    barrier = pltpu.get_barrier_semaphore()

    def signal(semaphore, device):
        pl.semaphore_signal(semaphore, inc=1, device_id=device, device_id_type=MESH)

    for load in loads[:3]:
        load.start()
    for _, device in plane_peers:
        signal(barrier, device)
    for z, device in z_peers:
        pl.when(z > my_z)(functools.partial(signal, barrier, device))
    for l, device in l_peers:
        pl.when(l > my_l)(functools.partial(signal, barrier, device))
    for load in loads[3:]:
        load.start()

    def remote(src, dst, send, recv, device):
        return pltpu.make_async_remote_copy(
            src_ref=src,
            dst_ref=dst,
            send_sem=send,
            recv_sem=recv,
            device_id=device,
            device_id_type=MESH,
        )

    n_owners = nq * nz
    n_slots = n_owners * CAP
    made = {}

    def assign_slots():
        marks[n_marks:, :] = jnp.zeros((128 - n_marks, depth), BF16)
        loads[2].wait()
        assigned = assign[...]
        owner, local = assigned // OWNED, assigned % OWNED
        hits = iota((n_owners, n_points), 0) == owner
        earlier = (iota((n_points, n_points), 0) < iota((n_points, n_points), 1)).astype(F32)
        before = dot(hits.astype(BF16), earlier.astype(BF16))
        rank = jnp.sum(jnp.where(hits, before, 0.0), axis=0, keepdims=True).astype(I32)
        owner_q = owner // (nz * 4) * 4 + owner % 4
        owner_z = owner // 4 % nz
        slot = (owner_z * nq + owner_q) * CAP + rank
        to_slot = (iota((n_slots, n_points), 0) == slot).astype(F32).astype(BF16)
        local_hot = (iota((128, n_points), 0) == local + n_marks).astype(F32).astype(BF16)
        made["to_slot"], made["ids"] = to_slot, dot(to_slot, local_hot, 1, 1)

    def kernel_rows():
        loads[0].wait()
        loads[1].wait()
        scores = dot(unit_rows(points[...]), unit_rows(marks[...]), 1, 1)
        rows = jnp.exp(scores * (0.5 / math.sqrt(depth)))
        made["rows"] = jnp.where(iota((n_points, 128), 1) < n_marks, rows, 0.0).astype(BF16)

    def fill_slots():
        filled = dot(made["to_slot"], made["rows"]) + made["ids"]
        slots[...] = filled.astype(BF16).reshape(nz, nq * CAP, 128)

    def everyone_in():
        pl.semaphore_wait(barrier, len(plane_peers) + my_z + my_l)
        for z, device in z_peers:
            pl.when(z < my_z)(functools.partial(signal, in_z.at[my_z], device))
        for l, device in l_peers:
            pl.when(l < my_l)(functools.partial(signal, in_l.at[my_l], device))

    sent = []

    def start(copies):
        for copy in copies:
            copy.start()
        sent.extend(copies)

    def core_copies(k):
        out, back = [], []
        for y in range(2):
            src, send, recv = half_of(mine, y, other_c, k), c1_send.at[k, y], c1_recv.at[k, y]
            out.append(remote(src, halves[k].at[my_c, y], send, recv, sibling))
            back.append(remote(src, halves[k].at[other_c, y], send, recv, sibling))
        return out, back

    def scatter_copies(k):
        out, back = [], []
        for x, y, device in xy_peers:
            src, at, dst = chosen[k].at[y, x], x * 2 + y, pieces[k]
            out.append(remote(src, dst.at[my_xy], p1_send.at[k, at], p1_recv.at[k, my_xy], device))
            back.append(remote(src, dst.at[at], p1_send.at[k, at], p1_recv.at[k, at], device))
        return out, back

    def gather_copies(k):
        out, back = [], []
        here = panel.at[my_c, my_xy, chunks[k]]
        for x, y, device in xy_peers:
            at = x * 2 + y
            there = panel.at[my_c, at, chunks[k]]
            out.append(remote(here, here, p3_send.at[k, at], p3_recv.at[k, my_xy], device))
            back.append(remote(there, there, p3_send.at[k, at], p3_recv.at[k, at], device))
        return out, back

    def share_copies(k):
        here, there = panel.at[my_c, :, chunks[k]], panel.at[other_c, :, chunks[k]]
        out = remote(here, here, c3_send.at[k], c3_recv.at[k], sibling)
        return [out], [remote(there, there, c3_send.at[k], c3_recv.at[k], sibling)]

    def z_copies(k):
        out, back = [], []
        for z, device in z_peers:
            here, there, send = planes[k].at[my_z], planes[k].at[z], p2_send.at[k, z]
            out.append(remote(here, here, send, p2_recv.at[k, my_z], device))
            back.append(remote(there, there, send, p2_recv.at[k, z], device))
        return out, back

    def arrive(copies):
        for copy in copies:
            copy.wait_recv()

    rz, rz_back, rq, rq_back, s, s_back = [], [], [], [], [], []
    for z, device in z_peers:
        rz.append(remote(slots.at[z], rows_z.at[my_z], rz_send.at[z], rz_recv.at[my_z], device))
        rz_back.append(remote(slots.at[z], rows_z.at[z], rz_send.at[z], rz_recv.at[z], device))
    for q, device in plane_peers:
        rq.append(remote(regrouped.at[q], rows_q.at[my_q], rq_send.at[q], rq_recv.at[my_q], device))
        rq_back.append(remote(regrouped.at[q], rows_q.at[q], rq_send.at[q], rq_recv.at[q], device))
    for l, device in l_peers:
        s.append(remote(sums.at[my_l], sums.at[my_l], s_send.at[l], s_recv.at[my_l], device))
        s_back.append(remote(sums.at[l], sums.at[l], s_send.at[l], s_recv.at[l], device))
    own_z = pltpu.make_async_copy(slots.at[my_z], rows_z.at[my_z], load_sem.at[4])
    own_q = pltpu.make_async_copy(regrouped.at[my_q], rows_q.at[my_q], load_sem.at[4])
    c1 = [core_copies(k) for k in range(CHUNKS)]
    p1 = [scatter_copies(k) for k in range(CHUNKS)]
    p2 = [z_copies(k) for k in range(CHUNKS)]
    p3 = [gather_copies(k) for k in range(CHUNKS)]
    c3 = [share_copies(k) for k in range(CHUNKS)]

    def to_sibling(k):
        if k == 0:
            loads[3].wait()
        start(c1[k][0])

    def source():
        holder = index_ref[0, 0]
        yc = holder % 4
        return yc % 2, holder // (nz * 4) * 2 + yc // 2, holder // 4 % nz

    def scatter(k):
        if k == 0:
            loads[4].wait()
        for y in range(2):
            loads[5 + 2 * k + y].wait()
        arrive(c1[k][1])
        chosen[k][...] = halves[k][source()[0]]
        pieces[k][my_xy] = chosen[k][my_y, my_x]
        start(p1[k][0])

    def along_z(k):
        arrive(p1[k][1])
        planes[k][my_z] = pieces[k][source()[1]]
        start(p2[k][0])

    def gather(k):
        arrive(p2[k][1])
        panel[my_c, my_xy, chunks[k]] = planes[k][source()[2]]
        start(p3[k][0])

    def share(k):
        arrive(p3[k][1])
        start(c3[k][0])

    def rows_down():
        own_z.start()
        for (z, _), copy in zip(z_peers, rz):
            pl.when(z < my_z)(copy.start)

    def rows_up():
        for (z, _), copy in zip(z_peers, rz):

            @pl.when(z > my_z)
            def _():
                pl.semaphore_wait(in_z.at[z], 1)
                copy.start()

        sent.extend(rz)

    def order_rows():
        target = iota((n_slots, n_slots), 0)
        at_q, at_z, at_r = target // (nz * CAP), target // CAP % nz, target % CAP
        regroup = iota((n_slots, n_slots), 1) == (at_z * nq + at_q) * CAP + at_r
        regroup = regroup.astype(F32).astype(BF16)
        made["regroup"] = regroup

    def rows_in_plane():
        own_z.wait()
        arrive(rz_back)
        grouped = dot(made["regroup"], rows_z[...].reshape(n_slots, 128)).astype(BF16)
        regrouped[...] = grouped.reshape(nq, nz * CAP, 128)
        start(rq)
        own_q.start()

    def sum_rows():
        own_q.wait()
        arrive(rq_back)
        received = rows_q[...].reshape(n_slots, 128)
        gram = dot(received, received, 0, 0)
        sums[my_l] = gram[n_marks:, :] * (OWNED * n_owners / (n_points * n_owners))
        for l, _ in l_peers:
            pl.when(l > my_l)(functools.partial(pl.semaphore_wait, in_l.at[l], 1))
        start(s)
        totals = dot(jnp.ones((8, n_slots), BF16), received)
        count_ref[...] = pltpu.roll(totals, 128 - n_marks, 1)[:1, :OWNED].astype(I32)

    def finish():
        arrive(s_back)
        factors = []
        for l in range(nl):
            whole = sums[l][:, :n_marks]
            high = whole.astype(BF16)
            low = (whole - high.astype(F32)).astype(BF16)
            factors.append(jnp.concatenate([high, low], axis=0))
        for k in range(CHUNKS):
            arrive(c3[k][1])
        for column in range(4):
            both = dot(factors[0], panel[column % 2, column // 2])
            for l in range(1, nl):
                both = both + dot(factors[l], panel[column % 2, l * 2 + column // 2])
            out_ref[:, column * 128 : (column + 1) * 128] = both[:OWNED] + both[OWNED:]

    assign_slots()
    kernel_rows()
    fill_slots()
    everyone_in()
    rows_down()
    for k in range(CHUNKS):
        to_sibling(k)
    for k in range(CHUNKS):
        scatter(k)
    rows_up()
    order_rows()
    for k in range(CHUNKS):
        along_z(k)
    rows_in_plane()
    gather(0)
    gather(1)
    sum_rows()
    gather(2)
    for k in range(CHUNKS):
        share(k)
    finish()
    for copy in sent:
        copy.wait_send()


def write_out(total, count, out_hbm, count_hbm, sems):
    copies = [
        pltpu.make_async_copy(total, out_hbm, sems.at[0]),
        pltpu.make_async_copy(count, count_hbm, sems.at[1]),
    ]
    for copy in copies:
        copy.start()
    for copy in copies:
        copy.wait()


def solution(mesh):
    pts, nl = mesh.shape["pts"], mesh.shape["lmk"]
    nx = nl
    nz = pts // (nx * 4)
    nq = nx * 4

    def body(points, landmarks, panels, panel_index, assignment):
        n_points, depth = points.shape
        n_marks = landmarks.shape[0]
        columns = panels.shape[2]
        step = n_marks // CHUNKS
        hbm = pl.BlockSpec(memory_space=pl.ANY)
        vmem = pl.BlockSpec(memory_space=pltpu.VMEM)
        dma = pltpu.SemaphoreType.DMA
        out, counts = pl.pallas_call(
            functools.partial(kernel, nx, nz, nl),
            out_shape=(
                pltpu.VMEM((OWNED, columns), F32),
                pltpu.VMEM((1, OWNED), I32),
            ),
            in_specs=[hbm] * 5,
            out_specs=(vmem, vmem),
            scratch_shapes=[
                pltpu.SMEM((1, 1), I32),
                pltpu.VMEM((n_points, depth), BF16),
                pltpu.VMEM((128, depth), BF16),
                pltpu.VMEM((1, n_points), I32),
                pltpu.VMEM((nl, n_marks, columns), BF16),
                [pltpu.VMEM((2, 2, nx, step, 128), BF16)] * CHUNKS,
                [pltpu.VMEM((2, nx, step, 128), BF16)] * CHUNKS,
                pltpu.VMEM((nz, nq * CAP, 128), BF16),
                pltpu.VMEM((nz, nq * CAP, 128), BF16),
                pltpu.VMEM((nq, nz * CAP, 128), BF16),
                pltpu.VMEM((nq, nz * CAP, 128), BF16),
                [pltpu.VMEM((nx * 2, step, 128), BF16)] * CHUNKS,
                [pltpu.VMEM((nz, step, 128), BF16)] * CHUNKS,
                pltpu.VMEM((2, nx * 2, n_marks, 128), BF16),
                pltpu.VMEM((nl, OWNED, 128), F32),
                dma((6 + 2 * CHUNKS,)),
                dma((nz,)),
                dma((nz,)),
                dma((nq,)),
                dma((nq,)),
                dma((CHUNKS, 2)),
                dma((CHUNKS, 2)),
                dma((CHUNKS, nx * 2)),
                dma((CHUNKS, nx * 2)),
                dma((CHUNKS, nz)),
                dma((CHUNKS, nz)),
                dma((CHUNKS, nx * 2)),
                dma((CHUNKS, nx * 2)),
                dma((CHUNKS,)),
                dma((CHUNKS,)),
                dma((nl,)),
                dma((nl,)),
                pltpu.SemaphoreType.REGULAR((nz,)),
                pltpu.SemaphoreType.REGULAR((nl,)),
            ],
            compiler_params=pltpu.CompilerParams(collective_id=0, has_side_effects=True),
        )(panel_index.reshape(1, 1), points, landmarks, panels.reshape(nl, n_marks, columns), assignment.reshape(1, n_points))
        out, counts = pl.pallas_call(
            write_out,
            out_shape=(
                jax.ShapeDtypeStruct((OWNED, columns), F32),
                jax.ShapeDtypeStruct((1, OWNED), I32),
            ),
            in_specs=[vmem, vmem],
            out_specs=(hbm, hbm),
            scratch_shapes=[dma((2,))],
        )(*(pltpu.with_memory_space_constraint(a, pltpu.VMEM) for a in (out, counts)))
        return out, counts.reshape(OWNED)

    in_specs = (P("pts", None), P("lmk", None), P("pts", None, "lmk"), P(), P("pts"))
    out_specs = (P("pts", "lmk"), P("pts"))
    return jax.shard_map(body, mesh=mesh, in_specs=in_specs, out_specs=out_specs, check_vma=False)
```
